128 devices in a mesh: pool: 32 (over y, x, core), head: 4 (over z).
Axes of the slice: x: 4, y: 4, z: 4, core: 2. Of those that a mesh axis runs over, the one named last changes fastest.
Arguments:
- x_rows: bfloat16 [1024, 4096], P('pool'), may hold values from -3 to 3
- query: bfloat16 [1024, 4096], P('pool', 'head'), may hold values from -170 to 170
- key_cache: bfloat16 [1024, 4, 512, 128], P('pool', 'head'), may hold values from -6 to 6
- value_cache: bfloat16 [1024, 4, 512, 128], P('pool', 'head'), may hold values from -6 to 6
- new_key: bfloat16 [1024, 512], P('pool', 'head'), may hold values from -6 to 6
- new_value: bfloat16 [1024, 512], P('pool', 'head'), may hold values from -6 to 6
- lengths: int32 [1024], P('pool'), may hold values from 2 to 512, as said below
- out_proj: bfloat16 [4096, 4096], P('head'), may hold values from -0.5 to 0.5
- norm_gain: float32 [4096], replicated, may hold values from 0.5 to 1.5
- expert_ids: int32 [1024, 8], P('pool'), may hold values from 0 to 63, all different within a row; in each aligned block of 32 rows (0 to 31, 32 to 63, ...) at most 8 rows name the same one
- gate_weights: float32 [1024, 8], P('pool'), may hold values from 0.05 to 1
- w_gate: bfloat16 [64, 4096, 1024], P('pool', None, 'head'), may hold values from -0.09375 to 0.09375
- w_up: bfloat16 [64, 4096, 1024], P('pool', None, 'head'), may hold values from -0.09375 to 0.09375
- w_down: bfloat16 [64, 1024, 4096], P('pool', 'head'), may hold values from -0.1875 to 0.1875
Outputs:
- layer_out: bfloat16 [1024, 4096], P('pool', 'head')
The draws below stay inside these ranges and needn't reach their ends.
Inputs may be any that keep to these rules, and one draw needn't show every extreme that they name: `expert_ids`: within the 32 requests of one index of pool, no expert is named by more than 8 pairs, a bound that some block reaches. `lengths`: request 0 uses all 512 slots.
All inputs are finite; a program needn't handle non-finite values.
Results may differ from the reference program's by a relative error of at most 0.017.
Values may be sent and summed in bfloat16 or wider, within the bound.
No kernel may reach another device: no remote copies, remote signals or barrier semaphores. Data moves between devices by JAX's collectives and lax.ppermute only.
A program may use at most 128 MiB of HBM per device.

```python
import math
import jax
import jax.numpy as jnp
import numpy as np
from jax import lax

D = 4096
HD = 128
KVH = 4
QPK = 8
EFF = 1024
TOP = 8
CTX = 512
REQ_DEV = 32
REQS = 1024
EXPERTS = 64
CAP = 8
MOST = 256


def cache_base(key):
    return jnp.clip(jax.random.normal(jax.random.fold_in(key, 101), (REQS, KVH, CTX, HD), jnp.float32), -6.0, 6.0)


def draw_key_cache(key, part):
    base_keys = cache_base(key)
    return base_keys.astype(jnp.bfloat16)


def draw_query(key, part):
    entries = jnp.clip(jax.random.normal(jax.random.fold_in(key, 202), (REQS, KVH, QPK, HD), jnp.float32), -6.0, 6.0)
    return entries.reshape(REQS, KVH * QPK * HD).astype(jnp.bfloat16)


def draw_lengths(key, part):
    drawn = jax.random.randint(jax.random.fold_in(key, 303), (REQS,), 2, CTX + 1, jnp.int32)
    return drawn.at[0].set(CTX)


def block_scale(own_key, dims, cuts, smallest, top_value):
    factor_of, own = 1.0, jax.random.fold_in(own_key, 6)
    for position, blocks in cuts:
        steps = jnp.exp(jax.random.uniform(jax.random.fold_in(own, position), (blocks,), jnp.float32, smallest / len(cuts), top_value / len(cuts)))
        factor_of = factor_of * jnp.repeat(steps, dims[position] // blocks).reshape([-1 if axis == position else 1 for axis in range(len(dims))])
    return factor_of


def deal_out(stream_key, own, number, rows, count, top, bound, skew):
    ranking = jax.random.permutation(stream_key, count)
    crowded, ordinary = portions_of(count, rows * top, bound, skew, True), portions_of(count, rows * top, bound, skew, False)
    places = jnp.arange(count)

    def named(sizes, turn):
        used = int((sizes > 0).sum())
        fixed = max(1, used // 4)
        shifted = fixed + (places - fixed + turn * (used - fixed)) % max(1, count - fixed)
        return jnp.zeros((count,), jnp.int32).at[ranking[jnp.where(places < fixed, places, shifted)]].set(jnp.asarray(sizes, jnp.int32))

    sizes = jnp.where(number % 4 == 0, named(crowded, number // 4), named(ordinary, number - number // 4 - 1))
    mixed = jax.random.permutation(jax.random.fold_in(own, 3), count)
    donor, receiver = mixed[0:count // 2 * 2:2], mixed[1:count // 2 * 2:2]
    room = jnp.minimum(sizes[donor] - 1, bound - sizes[receiver]) // 2
    room = jnp.where((donor == ranking[0]) | (receiver == ranking[0]) | (sizes[receiver] == 0), 0, jnp.maximum(room, 0))
    shifted = jax.random.randint(jax.random.fold_in(own, 4), (count // 2,), 0, 1 << 20) % (room + 1)
    sizes = sizes.at[donor].add(-shifted).at[receiver].add(shifted)
    members = jnp.searchsorted(jnp.cumsum(sizes), jnp.arange(rows * top), side="right").astype(jnp.int32)
    grid = members.reshape(top, rows).T
    grid = grid[jax.random.permutation(jax.random.fold_in(own, 1), rows)]
    turn = jax.random.randint(jax.random.fold_in(own, 2), (rows, 1), 0, top)
    return jnp.take_along_axis(grid, (jnp.arange(top)[None, :] + turn) % top, axis=1)


def portions_of(number_of, total, bound, slope, full):
    weights = [(1 << 20) // math.isqrt(rank ** slope) + 1 for rank in range(1, number_of + 1)]
    largest = bound if full else min(bound, max(-(-total // number_of), total * weights[0] // sum(weights)))
    least = 1 if total - largest >= number_of - 1 else 0
    holding, spare = [largest] + [least] * (number_of - 1), total - largest - least * (number_of - 1)
    while spare > 0:
        free = [i for i in range(1, number_of) if holding[i] < largest] or [i for i in range(1, number_of) if holding[i] < bound]
        mass, budget = sum([weights[i] for i in free]), spare
        for i in free:
            more = min(bound - holding[i], max(1, budget * weights[i] // mass), spare)
            holding[i] = holding[i] + more
            spare = spare - more
    return np.array(holding)


def bell_draw(rng, dims, deviation, limit, cuts=(), kind=jnp.bfloat16):
    factor_of = block_scale(rng, dims, cuts, -0.22, 0.18) if cuts else 1.0
    array = jax.random.normal(rng, dims, jnp.float32) * deviation * factor_of
    return jnp.minimum(jnp.maximum(array, -limit), limit).astype(kind)


def setup_inputs(seed: int = 0) -> dict:
    keys = jax.random.split(jax.random.key(seed), 15)
    x_rows = bell_draw(keys[0], (REQS, D), 0.5, 3.0, ((0, 32),))
    query = draw_query(jax.random.fold_in(keys[14], 71), 0)
    key_cache = draw_key_cache(jax.random.fold_in(keys[14], 71), 0)
    value_cache = bell_draw(keys[3], (REQS, KVH, CTX, HD), 1.0, 6.0, ((0, 32), (1, 4)))
    new_key = bell_draw(keys[4], (REQS, KVH * HD), 1.0, 6.0, ((0, 32), (1, 4)))
    new_value = bell_draw(keys[5], (REQS, KVH * HD), 1.0, 6.0, ((0, 32), (1, 4)))
    lengths = draw_lengths(jax.random.fold_in(keys[14], 71), 0)
    out_proj = bell_draw(keys[7], (KVH * QPK * HD, D), HD ** -0.5, 0.5, ((0, 4),))
    norm_gain = jnp.clip(1.0 + 0.1 * jax.random.normal(keys[8], (D,), jnp.float32), 0.5, 1.5)
    expert_ids_keys = jax.random.split(jax.random.fold_in(keys[9], 1), REQS // REQ_DEV)
    expert_ids_turns = jax.random.permutation(jax.random.fold_in(keys[9], 3), REQS // REQ_DEV)
    expert_ids = jax.vmap(lambda own, number: deal_out(jax.random.fold_in(keys[9], 2), own, number, REQ_DEV, EXPERTS, TOP, CAP, 2))(expert_ids_keys, expert_ids_turns).reshape((REQS, TOP))
    gate_weights = jnp.clip(jnp.exp(math.log(1.0) - 2.9957323 * jax.random.uniform(keys[10], (REQS, TOP), jnp.float32) ** block_scale(keys[10], (REQS, TOP), ((0, 32),), -0.2, 0.2)), 0.05, 1.0)
    w_gate = bell_draw(keys[11], (EXPERTS, D, EFF), D ** -0.5, 0.09375, ((0, 32), (2, 4)))
    w_up = bell_draw(keys[12], (EXPERTS, D, EFF), D ** -0.5, 0.09375, ((0, 32), (2, 4)))
    w_down = bell_draw(keys[13], (EXPERTS, EFF, D), EFF ** -0.5, 0.1875, ((0, 32), (1, 4)))
    return {"x_rows": x_rows, "query": query, "key_cache": key_cache, "value_cache": value_cache, "new_key": new_key, "new_value": new_value, "lengths": lengths, "out_proj": out_proj, "norm_gain": norm_gain, "expert_ids": expert_ids, "gate_weights": gate_weights, "w_gate": w_gate, "w_up": w_up, "w_down": w_down}


def reference(x_rows, query, key_cache, value_cache, new_key, new_value, lengths, out_proj, norm_gain, expert_ids, gate_weights, w_gate, w_up, w_down):
    score_scale = HD ** (-0.5)
    queries = query.reshape(REQS, KVH, QPK, HD).astype(jnp.float32)
    cached_keys = key_cache.astype(jnp.float32)
    cached_values = value_cache.astype(jnp.float32)
    scores = jnp.einsum('rhqd,rhcd->rhqc', queries, cached_keys) * score_scale
    fresh_score = jnp.einsum('rhqd,rhd->rhq', queries, new_key.reshape(REQS, KVH, HD).astype(jnp.float32)) * score_scale
    live_mask = (jnp.arange(CTX)[None, :] < lengths[:, None])[:, None, None, :]
    scores = jnp.where(live_mask, scores, -1e+30)
    highest = jnp.maximum(lax.optimization_barrier(jnp.max(scores, -1)), fresh_score)
    weights = jnp.where(live_mask, jnp.exp(scores - highest[..., None]), 0.0)
    own_term = jnp.exp(fresh_score - highest)
    totals = lax.optimization_barrier(jnp.sum(weights, -1)) + own_term
    probs = lax.optimization_barrier((weights / totals[..., None]).astype(jnp.bfloat16)).astype(jnp.float32)
    own_prob = lax.optimization_barrier((own_term / totals).astype(jnp.bfloat16)).astype(jnp.float32)
    mixed = jnp.einsum('rhqc,rhcd->rhqd', probs, cached_values)
    mixed = mixed + own_prob[..., None] * new_value.reshape(REQS, KVH, 1, HD).astype(jnp.float32)
    attn = mixed.astype(jnp.bfloat16).reshape(REQS, KVH * QPK * HD)
    hidden = x_rows.astype(jnp.float32) + jnp.dot(attn, out_proj, preferred_element_type=jnp.float32)
    mean_square = lax.optimization_barrier(jnp.mean(hidden * hidden, -1, keepdims=True))
    normed = (hidden * lax.rsqrt(mean_square + 1e-06) * norm_gain.astype(jnp.float32)[None, :]).astype(jnp.bfloat16)

    def one_expert(moe_sum, bundle):
        gate_mat, up_mat, down_mat, expert_index = bundle
        chosen_pair = expert_ids == expert_index
        chosen_row = jnp.any(chosen_pair, -1)
        row_weight = lax.optimization_barrier(jnp.sum(jnp.where(chosen_pair, gate_weights, 0.0), -1))
        picked_rows = jnp.nonzero(chosen_row, size=MOST, fill_value=0)[0].astype(jnp.int32)
        valid_rows = jnp.arange(MOST) < jnp.sum(chosen_row.astype(jnp.int32))
        picked = normed[picked_rows]
        gate_part = jnp.dot(picked, gate_mat, preferred_element_type=jnp.float32)
        up_part = jnp.dot(picked, up_mat, preferred_element_type=jnp.float32)
        act = (jax.nn.silu(gate_part) * up_part).astype(jnp.bfloat16)
        produced = lax.optimization_barrier(jnp.dot(act, down_mat, preferred_element_type=jnp.float32).astype(jnp.bfloat16)).astype(jnp.float32)
        scaled = produced * jnp.where(valid_rows, row_weight[picked_rows], 0.0)[:, None]
        return (moe_sum.at[picked_rows].add(scaled), None)
    start = jnp.zeros((REQS, D), jnp.float32)
    moe_sum, unused = lax.scan(one_expert, start, (w_gate, w_up, w_down, jnp.arange(EXPERTS).astype(jnp.int32)))
    return (hidden + moe_sum).astype(jnp.bfloat16)
```

```python
import jax
import jax.numpy as jnp
from jax import lax
from jax.sharding import PartitionSpec as P

F32 = jnp.float32
BF16 = jnp.bfloat16


def attend(query, key_cache, value_cache, new_key, new_value, lengths):
    token_count = query.shape[0]
    head_size = new_key.shape[1]
    queries = query.reshape(token_count, -1, head_size)
    cached_keys = key_cache[:, 0]
    cached_values = value_cache[:, 0]
    score_scale = head_size ** (-0.5)
    scores = (
        jnp.einsum("rqd,rcd->rqc", queries, cached_keys, preferred_element_type=jnp.float32)
        * score_scale
    )
    fresh_score = (
        jnp.einsum("rqd,rd->rq", queries, new_key, preferred_element_type=jnp.float32) * score_scale
    )
    live_mask = (jnp.arange(cached_keys.shape[1])[None, :] < lengths[:, None])[:, None, :]
    scores = jnp.where(live_mask, scores, -1e30)
    highest = jnp.maximum(jnp.max(scores, -1), fresh_score)
    weights = jnp.where(live_mask, jnp.exp(scores - highest[..., None]), 0.0)
    own_term = jnp.exp(fresh_score - highest)
    totals = jnp.sum(weights, -1) + own_term
    probs = (weights / totals[..., None]).astype(jnp.bfloat16)
    own_prob = (own_term / totals).astype(jnp.bfloat16)
    mixed = jnp.einsum("rqc,rcd->rqd", probs, cached_values, preferred_element_type=jnp.float32)
    mixed = (
        mixed + own_prob.astype(jnp.float32)[..., None] * new_value.astype(jnp.float32)[:, None, :]
    )
    return mixed.astype(jnp.bfloat16).reshape(token_count, -1)


def route_slots(expert_ids, capacity):
    flat = expert_ids.reshape(-1)
    count = flat.shape[0]
    order = jnp.arange(count)
    earlier = (flat[:, None] == flat[None, :]) & (order[None, :] < order[:, None])
    rank = jnp.sum(earlier.astype(jnp.int32), 1)
    return (flat * capacity + rank).reshape(expert_ids.shape)


def head_scatter_sum(terms, groups):
    share = terms.shape[1] // groups
    me = lax.axis_index("head")
    total = lax.dynamic_slice_in_dim(terms, me * share, share, 1)
    total = total.astype(F32)
    rounded = terms.astype(BF16)
    for step in range(1, groups):
        to = lax.rem(me + step, groups)
        piece = lax.dynamic_slice_in_dim(rounded, to * share, share, 1)
        got = lax.ppermute(piece, "head", [(i, (i + step) % groups) for i in range(groups)])
        total = total + got.astype(F32)
    return total


def body(
    x_rows,
    query,
    key_cache,
    value_cache,
    new_key,
    new_value,
    lengths,
    out_proj,
    norm_gain,
    expert_ids,
    gate_weights,
    w_gate,
    w_up,
    w_down,
):
    pools = lax.axis_size("pool")
    groups = lax.axis_size("head")
    rows, width = x_rows.shape
    share = width // groups
    local_experts = w_gate.shape[0]
    hidden_units = w_gate.shape[2]
    all_experts = pools * local_experts
    capacity = max(2, 2 * expert_ids.shape[0] * expert_ids.shape[1] // all_experts)
    slots = local_experts * capacity
    offset = lax.axis_index("head") * share

    attn = attend(query, key_cache, value_cache, new_key, new_value, lengths)
    terms = jnp.dot(attn, out_proj, preferred_element_type=F32)

    slot = route_slots(expert_ids, capacity)
    matching = jnp.arange(pools * slots)[:, None, None] == slot[None, :, :]
    send_table = jnp.sum(matching.astype(F32), 2).astype(BF16)
    take = jnp.sum(jnp.where(matching, gate_weights[None, :, :], 0.0), 2).T

    summed = head_scatter_sum(terms, groups)
    hidden = lax.dynamic_slice_in_dim(x_rows, offset, share, 1).astype(F32) + summed
    gain = lax.dynamic_slice_in_dim(norm_gain, offset, share, 0)
    scaled = (hidden * gain[None, :]).astype(BF16)
    outgoing = jnp.dot(send_table, scaled, preferred_element_type=F32).astype(BF16)
    outgoing = jnp.broadcast_to(
        outgoing.reshape(pools, 1, slots, share), (pools, groups, slots, share)
    ).reshape(pools * groups, slots, share)
    arrived = lax.all_to_all(outgoing, ("pool", "head"), split_axis=0, concat_axis=0, tiled=True)
    arrived = arrived.reshape(pools, groups, local_experts, capacity, share)

    gain_parts = norm_gain.reshape(groups, share)
    plain = arrived.astype(F32) / gain_parts[None, :, None, None, :]
    mean_square = jnp.sum(plain * plain, (1, 4)) / width
    inverse = lax.rsqrt(mean_square + 1e-06)
    inverse = inverse.transpose(1, 0, 2).reshape(local_experts, pools * capacity, 1)
    picked = arrived.transpose(2, 0, 3, 1, 4).reshape(local_experts, pools * capacity, width)
    gate_part = jnp.einsum("end,edf->enf", picked, w_gate, preferred_element_type=F32) * inverse
    up_part = jnp.einsum("end,edf->enf", picked, w_up, preferred_element_type=F32) * inverse
    act = (jax.nn.silu(gate_part) * up_part).astype(BF16)
    produced = jnp.einsum("enf,efd->end", act, w_down, preferred_element_type=F32).astype(BF16)
    produced = produced.reshape(local_experts, pools, capacity, groups, share)
    produced = produced.transpose(1, 3, 0, 2, 4).reshape(pools * groups, slots, share)
    returned = lax.all_to_all(produced, ("pool", "head"), split_axis=0, concat_axis=0, tiled=True)
    returned = returned.reshape(pools * groups * slots, share)
    take_all = jnp.broadcast_to(
        take.reshape(rows, pools, 1, slots), (rows, pools, groups, slots)
    ).reshape(rows, -1)
    take_high = take_all.astype(BF16)
    take_low = (take_all - take_high.astype(F32)).astype(BF16)
    moe = jnp.dot(take_high, returned, preferred_element_type=F32) + jnp.dot(
        take_low, returned, preferred_element_type=F32
    )
    return (hidden + moe).astype(BF16)


def solution(mesh):
    placed = (
        P("pool", None),
        P("pool", "head"),
        P("pool", "head", None, None),
        P("pool", "head", None, None),
        P("pool", "head"),
        P("pool", "head"),
        P("pool"),
        P("head", None),
        P(),
        P("pool", None),
        P("pool", None),
        P("pool", None, "head"),
        P("pool", None, "head"),
        P("pool", "head", None),
    )
    return jax.shard_map(
        body, mesh=mesh, in_specs=placed, out_specs=P("pool", "head"), check_vma=False
    )
```

```python
import functools

import jax
import jax.numpy as jnp
from jax import lax
from jax.experimental import pallas as pl
from jax.experimental.pallas import tpu as pltpu
from jax.sharding import PartitionSpec as P

F32 = jnp.float32
BF16 = jnp.bfloat16
GROUP = 8


def attend_kernel(lengths, q_ref, k_ref, v_ref, nk_ref, nv_ref, proj_hbm, out_ref, rows_ref, proj_ref, sems):
    step = pl.program_id(0)
    steps = pl.num_programs(0)
    parts = sems.shape[0]
    depth = proj_ref.shape[0] // parts

    def part(i):
        cut = pl.ds(i * depth, depth)
        return pltpu.make_async_copy(proj_hbm.at[cut], proj_ref.at[cut], sems.at[i])

    @pl.when(step == 0)
    def _():
        for i in range(parts):
            part(i).start()

    size = nk_ref.shape[1]
    heads = q_ref.shape[1] // size
    slots = k_ref.shape[2]
    scale = size ** (-0.5)
    base = pl.multiple_of(step * GROUP, GROUP)
    queries = q_ref[pl.ds(base, GROUP), :].astype(F32)
    new_keys = nk_ref[pl.ds(base, GROUP), :].astype(F32)
    new_values = nv_ref[pl.ds(base, GROUP), :].astype(F32)
    place = lax.broadcasted_iota(jnp.int32, (heads, slots), 1)
    done = []
    for j in range(GROUP):
        query = jnp.concatenate(
            [queries[j : j + 1, i * size : (i + 1) * size] for i in range(heads)], 0
        )
        scores = (
            lax.dot_general(
                query.astype(BF16),
                k_ref[j, 0],
                (((1,), (1,)), ((), ())),
                preferred_element_type=F32,
            )
            * scale
        )
        fresh = jnp.sum(query * new_keys[j : j + 1], 1, keepdims=True) * scale
        live = place < lengths[base + j]
        scores = jnp.where(live, scores, -1e30)
        highest = jnp.maximum(jnp.max(scores, 1, keepdims=True), fresh)
        weights = jnp.where(live, jnp.exp(scores - highest), 0.0)
        own = jnp.exp(fresh - highest)
        total = jnp.sum(weights, 1, keepdims=True) + own
        share = 1.0 / total
        probs = (weights * share).astype(BF16)
        own = (own * share).astype(BF16).astype(F32)
        mixed = jnp.dot(probs, v_ref[j, 0], preferred_element_type=F32)
        mixed = mixed + own * new_values[j : j + 1]
        done.append(jnp.concatenate([mixed[i : i + 1] for i in range(heads)], 1))
    rows_ref[pl.ds(base, GROUP), :] = jnp.concatenate(done, 0)

    @pl.when(step == steps - 1)
    def _():
        attn = rows_ref[...].astype(BF16)
        total = jnp.zeros(out_ref.shape, F32)
        for i in range(parts):
            part(i).wait()
        for i in range(parts):
            cut = slice(i * depth, (i + 1) * depth)
            total = total + jnp.dot(attn[:, cut], proj_ref[cut, :], preferred_element_type=F32)
        out_ref[...] = total.astype(out_ref.dtype)


def attend_project(query, key_cache, value_cache, new_key, new_value, lengths, out_proj):
    rows, wide = query.shape
    size = new_key.shape[1]
    slots = key_cache.shape[2]
    width = out_proj.shape[1]
    whole = lambda shape: pl.BlockSpec(shape, lambda s, n: (0, 0))
    cache = pl.BlockSpec((GROUP, 1, slots, size), lambda s, n: (s, 0, 0, 0))
    return pl.pallas_call(
        attend_kernel,
        out_shape=jax.ShapeDtypeStruct((rows, width), BF16),
        grid_spec=pltpu.PrefetchScalarGridSpec(
            num_scalar_prefetch=1,
            grid=(rows // GROUP,),
            in_specs=[
                whole((rows, wide)),
                cache,
                cache,
                whole((rows, size)),
                whole((rows, size)),
                pl.BlockSpec(memory_space=pl.ANY),
            ],
            out_specs=whole((rows, width)),
            scratch_shapes=[
                pltpu.VMEM((rows, wide), F32),
                pltpu.VMEM(out_proj.shape, BF16),
                pltpu.SemaphoreType.DMA((4,)),
            ],
        ),
        compiler_params=pltpu.CompilerParams(
            dimension_semantics=("arbitrary",), vmem_limit_bytes=40 << 20
        ),
        name="attend_project",
    )(lengths, query, key_cache, value_cache, new_key, new_value, out_proj)


def gate_up_kernel(x_ref, gate_ref, up_ref, act_ref, gate_sum, up_sum):
    step = pl.program_id(1)

    @pl.when(step == 0)
    def _():
        gate_sum[...] = jnp.zeros_like(gate_sum)
        up_sum[...] = jnp.zeros_like(up_sum)

    rows = gate_sum.shape[0]
    x = x_ref[...].reshape(rows, x_ref.shape[2])
    gate_sum[...] += jnp.dot(x, gate_ref[0], preferred_element_type=F32)
    up_sum[...] += jnp.dot(x, up_ref[0], preferred_element_type=F32)

    @pl.when(step == pl.num_programs(1) - 1)
    def _():
        gate = gate_sum[...]
        act_ref[0] = (gate / (1.0 + jnp.exp(-gate)) * up_sum[...]).astype(act_ref.dtype)


def gate_up(arrived, w_gate, w_up, capacity):
    pools, _, width = arrived.shape
    experts, _, units = w_gate.shape
    rows = pools * capacity
    depth = width // 4
    weight = pl.BlockSpec((1, depth, units), lambda e, k: (e, k, 0))
    return pl.pallas_call(
        gate_up_kernel,
        out_shape=jax.ShapeDtypeStruct((experts, rows, units), BF16),
        grid=(experts, width // depth),
        in_specs=[
            pl.BlockSpec((pools, capacity, depth), lambda e, k: (0, e, k)),
            weight,
            weight,
        ],
        out_specs=pl.BlockSpec((1, rows, units), lambda e, k: (e, 0, 0)),
        scratch_shapes=[pltpu.VMEM((rows, units), F32), pltpu.VMEM((rows, units), F32)],
        compiler_params=pltpu.CompilerParams(dimension_semantics=("arbitrary", "arbitrary")),
        name="gate_up",
    )(arrived, w_gate, w_up)


def down_kernel(*refs):
    *ins, out_ref = refs
    count = len(ins) // 2
    total = 0.0
    for act_ref, weight_ref in zip(ins[:count], ins[count:]):
        total = total + jnp.dot(act_ref[0], weight_ref[0], preferred_element_type=F32)
    out_ref[...] = total.astype(out_ref.dtype).reshape(out_ref.shape)


def down(acts, weights, pools, capacity):
    experts, rows, units = acts[0].shape
    share = weights[0].shape[2]
    return pl.pallas_call(
        down_kernel,
        out_shape=jax.ShapeDtypeStruct((pools, experts * capacity, share), BF16),
        grid=(experts,),
        in_specs=[pl.BlockSpec((1, rows, units), lambda e: (e, 0, 0))] * len(acts)
        + [pl.BlockSpec((1, units, share), lambda e: (e, 0, 0))] * len(weights),
        out_specs=pl.BlockSpec((pools, capacity, share), lambda e: (0, e, 0)),
        compiler_params=pltpu.CompilerParams(dimension_semantics=("arbitrary",)),
        name="down",
    )(*acts, *weights)


def route_slots(expert_ids, capacity):
    flat = expert_ids.reshape(-1)
    order = jnp.arange(flat.shape[0])
    earlier = (flat[:, None] == flat[None, :]) & (order[None, :] < order[:, None])
    rank = jnp.sum(earlier.astype(jnp.int32), 1)
    return (flat * capacity + rank).reshape(expert_ids.shape)


def turned(value, step):
    groups = lax.axis_size("head")
    return lax.ppermute(value, "head", [(i, (i + step) % groups) for i in range(groups)])


def body(
    x_rows,
    query,
    key_cache,
    value_cache,
    new_key,
    new_value,
    lengths,
    out_proj,
    norm_gain,
    expert_ids,
    gate_weights,
    w_gate,
    w_up,
    w_down,
):
    pools = lax.axis_size("pool")
    groups = lax.axis_size("head")
    rows, width = x_rows.shape
    share = width // groups
    experts = w_gate.shape[0]
    capacity = max(2, 2 * expert_ids.shape[0] * expert_ids.shape[1] // (pools * experts))
    slots = experts * capacity
    head = lax.axis_index("head")
    steps = range(1, groups)

    terms = attend_project(query, key_cache, value_cache, new_key, new_value, lengths, out_proj)
    with jax.named_scope("terms"):
        others = [turned(terms, step) for step in steps]

    slot = route_slots(expert_ids, capacity)
    matching = jnp.arange(pools * slots)[:, None, None] == slot[None, :, :]
    send_table = jnp.sum(matching.astype(F32), 2).astype(BF16)
    take = jnp.sum(jnp.where(matching, gate_weights[None, :, :], 0.0), 2).T
    take_high = take.astype(BF16)
    take_low = (take - take_high.astype(F32)).astype(BF16)
    columns = [
        lax.dynamic_slice_in_dim(w_down, lax.rem(head + step, groups) * share, share, 2)
        for step in range(groups)
    ]

    hidden = x_rows.astype(F32) + terms.astype(F32)
    for other in others:
        hidden = hidden + other.astype(F32)
    mean_square = jnp.mean(hidden * hidden, -1, keepdims=True)
    normed = (hidden * lax.rsqrt(mean_square + 1e-06) * norm_gain[None, :]).astype(BF16)
    kept = lax.dynamic_slice_in_dim(hidden, head * share, share, 1)
    *sent, normed = lax.optimization_barrier((*columns[1:], normed))
    with jax.named_scope("weights"):
        moved = [turned(piece, step) for step, piece in zip(steps, sent)]
    with jax.named_scope("dispatch"):
        outgoing = jnp.dot(send_table, normed, preferred_element_type=F32).astype(BF16)
        outgoing = outgoing.reshape(pools, slots, width)
        arrived = lax.all_to_all(outgoing, "pool", split_axis=0, concat_axis=0, tiled=True)

    act = gate_up(arrived, w_gate, w_up, capacity)
    with jax.named_scope("acts"):
        acts = [act] + [turned(act, step) for step in steps]
    produced = down(acts, [columns[0]] + moved, pools, capacity)
    with jax.named_scope("return"):
        returned = lax.all_to_all(produced, "pool", split_axis=0, concat_axis=0, tiled=True)
    returned = returned.reshape(pools * slots, share)
    moe = jnp.dot(take_high, returned, preferred_element_type=F32) + jnp.dot(
        take_low, returned, preferred_element_type=F32
    )
    return (kept + moe).astype(BF16)


def solution(mesh):
    placed = (
        P("pool", None),
        P("pool", "head"),
        P("pool", "head", None, None),
        P("pool", "head", None, None),
        P("pool", "head"),
        P("pool", "head"),
        P("pool"),
        P("head", None),
        P(),
        P("pool", None),
        P("pool", None),
        P("pool", None, "head"),
        P("pool", None, "head"),
        P("pool", "head", None),
    )
    return jax.shard_map(
        body, mesh=mesh, in_specs=placed, out_specs=P("pool", "head"), check_vma=False
    )
```

```python
import jax
import jax.numpy as jnp
from jax import lax
from jax.experimental import pallas as pl
from jax.experimental.pallas import tpu as pltpu
from jax.sharding import PartitionSpec as P

F32 = jnp.float32
BF16 = jnp.bfloat16
GROUP = 8
HEAD, ROW, COLUMN, CORE = range(4)


def attend_kernel(lengths, place, q_ref, k_ref, v_ref, nk_ref, nv_ref, proj_hbm, *outs):
    *out_refs, rows_ref, proj_ref, sems = outs
    step = pl.program_id(0)
    steps = pl.num_programs(0)
    parts = sems.shape[0]
    depth = proj_ref.shape[0] // parts

    def part(i):
        cut = pl.ds(i * depth, depth)
        return pltpu.make_async_copy(proj_hbm.at[cut], proj_ref.at[cut], sems.at[i])

    @pl.when(step == 0)
    def _():
        for i in range(parts):
            part(i).start()

    size = nk_ref.shape[1]
    heads = q_ref.shape[1] // size
    slots = k_ref.shape[2]
    scale = size ** (-0.5)
    base = pl.multiple_of(step * GROUP, GROUP)
    queries = q_ref[pl.ds(base, GROUP), :].astype(F32)
    new_keys = nk_ref[pl.ds(base, GROUP), :].astype(F32)
    new_values = nv_ref[pl.ds(base, GROUP), :].astype(F32)
    slot_of = lax.broadcasted_iota(jnp.int32, (heads, slots), 1)
    done = []
    blank = jnp.zeros((heads, size), F32)
    for j in range(0, GROUP, 2):
        pair = [
            jnp.concatenate([queries[k : k + 1, i * size : (i + 1) * size] for i in range(heads)], 0)
            for k in (j, j + 1)
        ]
        spread = jnp.concatenate(
            [jnp.concatenate([pair[0], blank], 1), jnp.concatenate([blank, pair[1]], 1)], 0
        )
        keys = jnp.concatenate([k_ref[j, 0], k_ref[j + 1, 0]], 1)
        values = jnp.concatenate([v_ref[j, 0], v_ref[j + 1, 0]], 1)
        scores = (
            lax.dot_general(
                spread.astype(BF16), keys, (((1,), (1,)), ((), ())), preferred_element_type=F32
            )
            * scale
        )
        fresh = [
            jnp.sum(pair[k] * new_keys[j + k : j + k + 1], 1, keepdims=True) for k in range(2)
        ]
        fresh = jnp.concatenate(fresh, 0) * scale
        live = jnp.concatenate([slot_of < lengths[base + j + k] for k in range(2)], 0)
        scores = jnp.where(live, scores, -1e30)
        highest = jnp.maximum(jnp.max(scores, 1, keepdims=True), fresh)
        weights = jnp.where(live, jnp.exp(scores - highest), 0.0)
        own = jnp.exp(fresh - highest)
        total = jnp.sum(weights, 1, keepdims=True) + own
        share = 1.0 / total
        probs = (weights * share).astype(BF16)
        own = (own * share).astype(BF16).astype(F32)
        mixed = jnp.dot(probs, values, preferred_element_type=F32)
        for k in range(2):
            rows = slice(k * heads, (k + 1) * heads)
            part_sum = mixed[rows, k * size : (k + 1) * size] + own[rows] * new_values[j + k : j + k + 1]
            done.append(jnp.concatenate([part_sum[i : i + 1] for i in range(heads)], 1))
    rows_ref[pl.ds(base, GROUP), :] = jnp.concatenate(done, 0)

    @pl.when(step == steps - 1)
    def _():
        attn = rows_ref[...].astype(BF16)
        for i in range(parts):
            part(i).wait()
        groups = len(out_refs)
        share = out_refs[0].shape[1]
        for ahead in [*range(1, groups), 0]:
            column = lax.rem(place[HEAD] + ahead, groups) * share
            weight = proj_ref[:, pl.ds(pl.multiple_of(column, share), share)]
            terms = jnp.dot(attn, weight, preferred_element_type=F32)
            out_refs[ahead][...] = terms.astype(out_refs[ahead].dtype)


def in_hbm(value):
    return pltpu.with_memory_space_constraint(value, pltpu.HBM)


def in_vmem(values):
    return [pltpu.with_memory_space_constraint(value, pltpu.VMEM) for value in values]


def attend_project(query, key_cache, value_cache, new_key, new_value, lengths, place, out_proj, groups):
    rows, wide = query.shape
    size = new_key.shape[1]
    slots = key_cache.shape[2]
    share = out_proj.shape[1] // groups
    whole = lambda shape: pl.BlockSpec(shape, lambda s, *_: (0, 0))
    cache = pl.BlockSpec((GROUP, 1, slots, size), lambda s, *_: (s, 0, 0, 0))
    return pl.pallas_call(
        attend_kernel,
        out_shape=[
            jax.ShapeDtypeStruct((rows, share), BF16 if ahead else F32) for ahead in range(groups)
        ],
        grid_spec=pltpu.PrefetchScalarGridSpec(
            num_scalar_prefetch=2,
            grid=(rows // GROUP,),
            in_specs=[
                whole((rows, wide)),
                cache,
                cache,
                whole((rows, size)),
                whole((rows, size)),
                pl.BlockSpec(memory_space=pl.ANY),
            ],
            out_specs=[whole((rows, share))] * groups,
            scratch_shapes=[
                pltpu.VMEM((rows, wide), F32),
                pltpu.VMEM(out_proj.shape, BF16),
                pltpu.SemaphoreType.DMA((4,)),
            ],
        ),
        compiler_params=pltpu.CompilerParams(
            dimension_semantics=("arbitrary",), vmem_limit_bytes=24 << 20
        ),
        name="attend_project",
    )(
        in_hbm(lengths),
        place,
        in_hbm(query),
        in_hbm(key_cache),
        in_hbm(value_cache),
        in_hbm(new_key),
        in_hbm(new_value),
        in_hbm(out_proj),
    )


def norm_kernel(place, own_ref, *refs):
    *other_refs, gain_ref, ids_ref, first_ref, second_ref = refs
    groups = 1 + len(other_refs)
    rows, share = own_ref.shape
    blocks = [own_ref[...]] + [ref[...].astype(F32) for ref in other_refs]
    square = sum(jnp.sum(block * block, 1, keepdims=True) for block in blocks)
    inverse = lax.rsqrt(square / (groups * share) + 1e-06)
    half = groups // 2
    for back, block in enumerate(blocks):
        gain = gain_ref[lax.rem(place[HEAD] + groups - back, groups)]
        out_ref = (first_ref, second_ref)[back // half]
        cut = (back % half) * share
        out_ref[:rows, cut : cut + share] = (block * inverse * gain).astype(BF16)
    for out_ref in (first_ref, second_ref):
        out_ref[rows:, :] = jnp.zeros((ids_ref.shape[0], half * share), BF16)
        out_ref[rows:, : ids_ref.shape[1]] = ids_ref[...]


def norm_rows(own, others, norm_gain, ids, place):
    rows, share = own.shape
    groups = 1 + len(others)
    gains = norm_gain.reshape(groups, 1, share)
    shape = jax.ShapeDtypeStruct((rows + ids.shape[0], groups // 2 * share), BF16)
    vmem = pl.BlockSpec(memory_space=pltpu.VMEM)
    return pl.pallas_call(
        norm_kernel,
        out_shape=[shape, shape],
        in_specs=[pl.BlockSpec(memory_space=pltpu.SMEM)] + [vmem] * (groups + 2),
        out_specs=[vmem, vmem],
        compiler_params=pltpu.CompilerParams(vmem_limit_bytes=8 << 20),
        name="norm_rows",
    )(place, *in_vmem([own, *others]), gains, ids)


def pick_kernel(place, *refs):
    count = 4
    pools = (place[ROW], place[COLUMN], place[CORE])
    slots, near, cores = refs[-1].shape[0], count, 2
    targets = count * cores
    depth = 32
    lanes = near * depth
    total = targets * slots
    line = lax.broadcasted_iota(jnp.int32, (total, lanes), 0)
    lane = lax.broadcasted_iota(jnp.int32, (total, lanes), 1)
    step, flip = line >> 7, (line >> 6) & 1
    expert, source, rank = (line >> 5) & 1, (line >> 3) & 3, line & 7
    core = pools[2] ^ flip
    upper_line = lax.broadcasted_iota(jnp.int32, (lanes, lanes), 0)
    upper_lane = lax.broadcasted_iota(jnp.int32, (lanes, lanes), 1)
    earlier = ((upper_line < upper_lane) & ((upper_line >> 5) == (upper_lane >> 5))).astype(F32)
    id_lane = lax.broadcasted_iota(jnp.int32, (8, lanes), 1) >> 5
    for half in range(2):
        ins = refs[half * near : (half + 1) * near]
        outs = refs[(2 + 2 * half) * near : (4 + 2 * half) * near]
        if half == 0:
            target = ((pools[0] + step) & 3) * 8 + pools[1] * 2 + core
        else:
            target = pools[0] * 8 + ((pools[1] + step) & 3) * 2 + core
        wanted = (target * 2 + expert).astype(F32)
        ids = jnp.zeros((8, lanes), F32)
        for back, ref in enumerate(ins):
            ids = jnp.where(id_lane == back, ref[depth:, :lanes].astype(F32), ids)
        hit = ids[0:1] == wanted
        for k in range(1, 8):
            hit = hit | (ids[k : k + 1] == wanted)
        hits = jnp.where(hit, 1.0, 0.0).astype(BF16)
        order = jnp.dot(hits, earlier.astype(BF16), preferred_element_type=F32)
        chosen = hit & (order == rank.astype(F32)) & ((lane >> 5) == source)
        table = jnp.where(chosen, 1.0, 0.0).astype(BF16)
        rows = jnp.concatenate([ref[:depth, :] for ref in ins], 0)
        picked = jnp.dot(table, rows, preferred_element_type=F32).astype(BF16)
        for i, out_ref in enumerate(outs):
            out_ref[...] = picked[i * slots : (i + 1) * slots]


def pick_rows(first, second, place):
    width = first[0].shape[1]
    shape = jax.ShapeDtypeStruct((64, width), BF16)
    vmem = pl.BlockSpec(memory_space=pltpu.VMEM)
    out = pl.pallas_call(
        pick_kernel,
        out_shape=[shape] * 16,
        in_specs=[pl.BlockSpec(memory_space=pltpu.SMEM)] + [vmem] * 8,
        out_specs=[vmem] * 16,
        compiler_params=pltpu.CompilerParams(vmem_limit_bytes=16 << 20),
        name="pick_rows",
    )(place, *in_vmem([*first, *second]))
    return out[:8], out[8:]


def gate_up_kernel(place, *refs):
    first, second = refs[:8], refs[8:16]
    gate_hbm, up_hbm, act_ref, weight_ref, sum_ref, sems = refs[16:]
    experts, groups, kinds, share, units = weight_ref.shape
    rows = act_ref.shape[1]

    def part(e, back, kind):
        cut = pl.ds(pl.multiple_of(lax.rem(place[HEAD] + groups - back, groups) * share, share), share)
        return pltpu.make_async_copy(
            (gate_hbm, up_hbm)[kind].at[e, cut], weight_ref.at[e, back, kind], sems.at[e, back, kind]
        )

    every = [(e, b, k) for e in range(experts) for b in range(groups) for k in range(kinds)]
    for which in every:
        part(*which).start()
    half = groups // 2
    for e in range(experts):
        sums = {}
        for back in range(groups):
            source = (first, second)[back // half]
            cut = slice((back % half) * share, (back % half + 1) * share)
            x = jnp.concatenate([ref[e * 32 : (e + 1) * 32, cut] for ref in source], 0)
            for kind in range(kinds):
                part(e, back, kind).wait()
                term = jnp.dot(x, weight_ref[e, back, kind], preferred_element_type=F32)
                key = (kind, back // half)
                sums[key] = sums[key] + term if key in sums else term
        for dy in range(4):
            for dc in range(2):
                for dx in range(4):
                    pool = (
                        ((place[ROW] + 4 - dy) & 3) * 8
                        + ((place[COLUMN] + 4 - dx) & 3) * 2
                        + (place[CORE] ^ dc)
                    )
                    a = ((dy * 2 + dc) * 4 + dx) * 8
                    b = ((dx * 2 + dc) * 4 + dy) * 8
                    for kind in range(kinds):
                        sum_ref[kind, pool] = (
                            sums[kind, 0][a : a + 8] + sums[kind, 1][b : b + 8]
                        )
        gate = sum_ref[0].reshape(rows, units)
        up = sum_ref[1].reshape(rows, units)
        act_ref[e] = (gate / (1.0 + jnp.exp(-gate)) * up).astype(act_ref.dtype)


def gate_up(first, second, w_gate, w_up, place, groups, pools, capacity):
    experts, width, units = w_gate.shape
    rows = pools * capacity
    share = width // groups
    vmem = pl.BlockSpec(memory_space=pltpu.VMEM)
    hbm = pl.BlockSpec(memory_space=pl.ANY)
    return pl.pallas_call(
        gate_up_kernel,
        out_shape=jax.ShapeDtypeStruct((experts, rows, units), BF16),
        in_specs=[pl.BlockSpec(memory_space=pltpu.SMEM)] + [vmem] * 16 + [hbm, hbm],
        out_specs=vmem,
        scratch_shapes=[
            pltpu.VMEM((experts, groups, 2, share, units), BF16),
            pltpu.VMEM((2, pools, capacity, units), F32),
            pltpu.SemaphoreType.DMA((experts, groups, 2)),
        ],
        compiler_params=pltpu.CompilerParams(vmem_limit_bytes=20 << 20),
        name="gate_up",
    )(place, *in_vmem([*first, *second]), in_hbm(w_gate), in_hbm(w_up))


def down_kernel(*refs):
    *ins, out_ref = refs
    count = len(ins) // 2
    total = 0.0
    for act_ref, weight_ref in zip(ins[:count], ins[count:]):
        total = total + jnp.dot(act_ref[0], weight_ref[0], preferred_element_type=F32)
    out_ref[...] = total.astype(out_ref.dtype).reshape(out_ref.shape)


def down(acts, weights, pools, capacity):
    experts, rows, units = acts[0].shape
    share = weights[0].shape[2]
    return pl.pallas_call(
        down_kernel,
        out_shape=jax.ShapeDtypeStruct((pools, experts * capacity, share), BF16),
        grid=(experts,),
        in_specs=[pl.BlockSpec((1, rows, units), lambda e: (e, 0, 0))] * len(acts)
        + [pl.BlockSpec((1, units, share), lambda e: (e, 0, 0))] * len(weights),
        out_specs=pl.BlockSpec((pools, capacity, share), lambda e: (0, e, 0)),
        compiler_params=pltpu.CompilerParams(
            dimension_semantics=("arbitrary",), vmem_limit_bytes=16 << 20
        ),
        name="down",
    )(*in_vmem([*acts, *weights]))


def route_slots(expert_ids, capacity):
    flat = expert_ids.reshape(-1)
    order = jnp.arange(flat.shape[0])
    earlier = (flat[:, None] == flat[None, :]) & (order[None, :] < order[:, None])
    rank = jnp.sum(earlier.astype(jnp.int32), 1)
    return (flat * capacity + rank).reshape(expert_ids.shape)


def turned(value, step):
    groups = lax.axis_size("head")
    return lax.ppermute(value, "head", [(i, (i + step) % groups) for i in range(groups)])


def moved_in_plane(value, dy, dx, dc):
    pairs = []
    for y in range(4):
        for x in range(4):
            for c in range(2):
                to = (y + dy) % 4 * 8 + (x + dx) % 4 * 2 + (c ^ dc)
                pairs.append((y * 8 + x * 2 + c, to))
    return lax.ppermute(value, "pool", pairs)


def body(
    x_rows,
    query,
    key_cache,
    value_cache,
    new_key,
    new_value,
    lengths,
    out_proj,
    norm_gain,
    expert_ids,
    gate_weights,
    w_gate,
    w_up,
    w_down,
):
    pools = lax.axis_size("pool")
    groups = lax.axis_size("head")
    rows, width = x_rows.shape
    share = width // groups
    experts = w_gate.shape[0]
    capacity = max(2, 2 * expert_ids.shape[0] * expert_ids.shape[1] // (pools * experts))
    slots = experts * capacity
    head = lax.axis_index("head")
    steps = range(1, groups)

    pool = lax.axis_index("pool")
    place = jnp.stack([head, pool >> 3, (pool >> 1) & 3, pool & 1]).astype(jnp.int32)
    own, *away = attend_project(
        query, key_cache, value_cache, new_key, new_value, lengths, place, out_proj, groups
    )
    with jax.named_scope("terms"):
        others = [turned(piece, step) for step, piece in zip(steps, away)]
    slot = route_slots(expert_ids, capacity)
    matching = jnp.arange(pools * slots)[:, None, None] == slot[None, :, :]
    take = jnp.sum(jnp.where(matching, gate_weights[None, :, :], 0.0), 2).T
    take_high = take.astype(BF16)
    take_low = (take - take_high.astype(F32)).astype(BF16)
    ids = jnp.tile(expert_ids.T.astype(BF16), (1, 128 // rows))
    columns = [
        lax.dynamic_slice_in_dim(w_down, lax.rem(head + step, groups) * share, share, 2)
        for step in range(groups)
    ]
    hidden = lax.dynamic_slice_in_dim(x_rows, head * share, share, 1).astype(F32) + own
    for other in others:
        hidden = hidden + other.astype(F32)
    with jax.named_scope("slices"):
        slices = [turned(hidden.astype(BF16), step) for step in steps]
    first, second = norm_rows(hidden, slices, norm_gain, ids, place)
    with jax.named_scope("near"):
        along_x = [first] + [moved_in_plane(first, 0, step, 0) for step in (1, 2, 3)]
        along_y = [second] + [moved_in_plane(second, step, 0, 0) for step in (1, 2, 3)]
    *sent, _ = lax.optimization_barrier((*columns[1:], first))
    with jax.named_scope("weights"):
        moved = [turned(piece, step) for step, piece in zip(steps, sent)]
    for_y, for_x = pick_rows(along_x, along_y, place)
    with jax.named_scope("far"):
        ways = [(step, flip) for step in range(4) for flip in range(2)]
        from_y = [
            moved_in_plane(value, step, 0, flip) if step or flip else value
            for value, (step, flip) in zip(for_y, ways)
        ]
        from_x = [
            moved_in_plane(value, 0, step, flip) if step or flip else value
            for value, (step, flip) in zip(for_x, ways)
        ]
    act = gate_up(from_y, from_x, w_gate, w_up, place, groups, pools, capacity)
    with jax.named_scope("acts"):
        acts = [act] + [turned(act, step) for step in steps]
    produced = down(acts, [columns[0]] + moved, pools, capacity)
    with jax.named_scope("return"):
        returned = lax.all_to_all(produced, "pool", split_axis=0, concat_axis=0, tiled=True)
    returned = returned.reshape(pools * slots, share)
    moe = jnp.dot(take_high, returned, preferred_element_type=F32) + jnp.dot(
        take_low, returned, preferred_element_type=F32
    )
    return (hidden + moe).astype(BF16)


def solution(mesh):
    placed = (
        P("pool", None),
        P("pool", "head"),
        P("pool", "head", None, None),
        P("pool", "head", None, None),
        P("pool", "head"),
        P("pool", "head"),
        P("pool"),
        P("head", None),
        P(),
        P("pool", None),
        P("pool", None),
        P("pool", None, "head"),
        P("pool", None, "head"),
        P("pool", "head", None),
    )
    return jax.shard_map(
        body, mesh=mesh, in_specs=placed, out_specs=P("pool", "head"), check_vma=False
    )
```

```python
import jax
import jax.numpy as jnp
from jax import lax
from jax.experimental import pallas as pl
from jax.experimental.pallas import tpu as pltpu
from jax.sharding import PartitionSpec as P


F32 = jnp.float32
BF16 = jnp.bfloat16
GROUP = 8
HEAD, ROW, COLUMN, CORE = range(4)
FAR_ORDER = ((2, 0), (2, 1), (1, 0), (3, 0), (1, 1), (3, 1), (0, 1))


def attend_kernel(lengths, place, q_ref, k_ref, v_ref, nk_ref, nv_ref, proj_hbm, *outs):
    *out_refs, rows_ref, proj_ref, sems = outs
    step = pl.program_id(0)
    steps = pl.num_programs(0)
    parts = sems.shape[0]
    depth = proj_ref.shape[0] // parts

    def part(i):
        cut = pl.ds(i * depth, depth)
        return pltpu.make_async_copy(proj_hbm.at[cut], proj_ref.at[cut], sems.at[i])

    @pl.when(step == 0)
    def _():
        for i in range(parts):
            part(i).start()

    size = nk_ref.shape[1]
    heads = q_ref.shape[1] // size
    slots = k_ref.shape[2]
    scale = size ** (-0.5)
    base = pl.multiple_of(step * GROUP, GROUP)
    queries = q_ref[pl.ds(base, GROUP), :].astype(F32)
    new_keys = nk_ref[pl.ds(base, GROUP), :].astype(F32)
    new_values = nv_ref[pl.ds(base, GROUP), :].astype(F32)
    slot_of = lax.broadcasted_iota(jnp.int32, (heads, slots), 1)
    done = []
    blank = jnp.zeros((heads, size), F32)
    for j in range(0, GROUP, 2):
        pair = [
            jnp.concatenate([queries[k : k + 1, i * size : (i + 1) * size] for i in range(heads)], 0)
            for k in (j, j + 1)
        ]
        spread = jnp.concatenate(
            [jnp.concatenate([pair[0], blank], 1), jnp.concatenate([blank, pair[1]], 1)], 0
        )
        keys = jnp.concatenate([k_ref[j, 0], k_ref[j + 1, 0]], 1)
        values = jnp.concatenate([v_ref[j, 0], v_ref[j + 1, 0]], 1)
        scores = (
            lax.dot_general(
                spread.astype(BF16), keys, (((1,), (1,)), ((), ())), preferred_element_type=F32
            )
            * scale
        )
        fresh = [
            jnp.sum(pair[k] * new_keys[j + k : j + k + 1], 1, keepdims=True) for k in range(2)
        ]
        fresh = jnp.concatenate(fresh, 0) * scale
        live = jnp.concatenate([slot_of < lengths[base + j + k] for k in range(2)], 0)
        scores = jnp.where(live, scores, -1e30)
        highest = jnp.maximum(jnp.max(scores, 1, keepdims=True), fresh)
        weights = jnp.where(live, jnp.exp(scores - highest), 0.0)
        own = jnp.exp(fresh - highest)
        total = jnp.sum(weights, 1, keepdims=True) + own
        share = 1.0 / total
        probs = (weights * share).astype(BF16)
        own = (own * share).astype(BF16).astype(F32)
        mixed = jnp.dot(probs, values, preferred_element_type=F32)
        for k in range(2):
            rows = slice(k * heads, (k + 1) * heads)
            part_sum = mixed[rows, k * size : (k + 1) * size] + own[rows] * new_values[j + k : j + k + 1]
            done.append(jnp.concatenate([part_sum[i : i + 1] for i in range(heads)], 1))
    rows_ref[pl.ds(base, GROUP), :] = jnp.concatenate(done, 0)

    @pl.when(step == steps - 1)
    def _():
        attn = rows_ref[...].astype(BF16)
        for i in range(parts):
            part(i).wait()
        groups = len(out_refs)
        share = out_refs[0].shape[1]
        for ahead in [*range(1, groups), 0]:
            column = lax.rem(place[HEAD] + ahead, groups) * share
            weight = proj_ref[:, pl.ds(pl.multiple_of(column, share), share)]
            terms = jnp.dot(attn, weight, preferred_element_type=F32)
            out_refs[ahead][...] = terms.astype(out_refs[ahead].dtype)


def in_hbm(value):
    return pltpu.with_memory_space_constraint(value, pltpu.HBM)


def in_vmem(values):
    return [pltpu.with_memory_space_constraint(value, pltpu.VMEM) for value in values]


def attend_project(query, key_cache, value_cache, new_key, new_value, lengths, place, out_proj, groups):
    rows, wide = query.shape
    size = new_key.shape[1]
    slots = key_cache.shape[2]
    share = out_proj.shape[1] // groups
    whole = lambda shape: pl.BlockSpec(shape, lambda s, *_: (0, 0))
    cache = pl.BlockSpec((GROUP, 1, slots, size), lambda s, *_: (s, 0, 0, 0))
    return pl.pallas_call(
        attend_kernel,
        out_shape=[
            jax.ShapeDtypeStruct((rows, share), BF16 if ahead else F32) for ahead in range(groups)
        ],
        grid_spec=pltpu.PrefetchScalarGridSpec(
            num_scalar_prefetch=2,
            grid=(rows // GROUP,),
            in_specs=[
                whole((rows, wide)),
                cache,
                cache,
                whole((rows, size)),
                whole((rows, size)),
                pl.BlockSpec(memory_space=pl.ANY),
            ],
            out_specs=[whole((rows, share))] * groups,
            scratch_shapes=[
                pltpu.VMEM((rows, wide), F32),
                pltpu.VMEM(out_proj.shape, BF16),
                pltpu.SemaphoreType.DMA((4,)),
            ],
        ),
        compiler_params=pltpu.CompilerParams(
            dimension_semantics=("arbitrary",), vmem_limit_bytes=24 << 20
        ),
        name="attend_project",
    )(
        in_hbm(lengths),
        place,
        in_hbm(query),
        in_hbm(key_cache),
        in_hbm(value_cache),
        in_hbm(new_key),
        in_hbm(new_value),
        in_hbm(out_proj),
    )


def norm_kernel(place, own_ref, *refs):
    *other_refs, gain_ref, ids_ref, first_ref, second_ref = refs
    groups = 1 + len(other_refs)
    rows, share = own_ref.shape
    blocks = [own_ref[...]] + [ref[...].astype(F32) for ref in other_refs]
    square = sum(jnp.sum(block * block, 1, keepdims=True) for block in blocks)
    inverse = lax.rsqrt(square / (groups * share) + 1e-06)
    half = groups // 2
    for back, block in enumerate(blocks):
        gain = gain_ref[lax.rem(place[HEAD] + groups - back, groups)]
        out_ref = (first_ref, second_ref)[back // half]
        cut = (back % half) * share
        out_ref[:rows, cut : cut + share] = (block * inverse * gain).astype(BF16)
    for out_ref in (first_ref, second_ref):
        out_ref[rows:, :] = jnp.zeros((ids_ref.shape[0], half * share), BF16)
        out_ref[rows:, : ids_ref.shape[1]] = ids_ref[...]


def norm_rows(own, others, norm_gain, ids, place):
    rows, share = own.shape
    groups = 1 + len(others)
    gains = norm_gain.reshape(groups, 1, share)
    shape = jax.ShapeDtypeStruct((rows + ids.shape[0], groups // 2 * share), BF16)
    vmem = pl.BlockSpec(memory_space=pltpu.VMEM)
    return pl.pallas_call(
        norm_kernel,
        out_shape=[shape, shape],
        in_specs=[pl.BlockSpec(memory_space=pltpu.SMEM)] + [vmem] * (groups + 2),
        out_specs=[vmem, vmem],
        compiler_params=pltpu.CompilerParams(vmem_limit_bytes=8 << 20),
        name="norm_rows",
    )(place, *in_vmem([own, *others]), gains, ids)


def pick_kernel(place, *refs):
    count = 4
    pools = (place[ROW], place[COLUMN], place[CORE])
    slots, near, cores = refs[-1].shape[0], count, 2
    targets = count * cores
    depth = 32
    lanes = near * depth
    total = targets * slots
    line = lax.broadcasted_iota(jnp.int32, (total, lanes), 0)
    lane = lax.broadcasted_iota(jnp.int32, (total, lanes), 1)
    step, flip = line >> 7, (line >> 6) & 1
    expert, source, rank = (line >> 5) & 1, (line >> 3) & 3, line & 7
    core = pools[2] ^ flip
    upper_line = lax.broadcasted_iota(jnp.int32, (lanes, lanes), 0)
    upper_lane = lax.broadcasted_iota(jnp.int32, (lanes, lanes), 1)
    earlier = ((upper_line < upper_lane) & ((upper_line >> 5) == (upper_lane >> 5))).astype(F32)
    id_lane = lax.broadcasted_iota(jnp.int32, (8, lanes), 1) >> 5
    for half in range(2):
        ins = refs[half * near : (half + 1) * near]
        outs = refs[(2 + 2 * half) * near : (4 + 2 * half) * near]
        if half == 0:
            target = ((pools[0] + step) & 3) * 8 + pools[1] * 2 + core
        else:
            target = pools[0] * 8 + ((pools[1] + step) & 3) * 2 + core
        wanted = (target * 2 + expert).astype(F32)
        ids = jnp.zeros((8, lanes), F32)
        for back, ref in enumerate(ins):
            ids = jnp.where(id_lane == back, ref[depth:, :lanes].astype(F32), ids)
        hit = ids[0:1] == wanted
        for k in range(1, 8):
            hit = hit | (ids[k : k + 1] == wanted)
        hits = jnp.where(hit, 1.0, 0.0).astype(BF16)
        order = jnp.dot(hits, earlier.astype(BF16), preferred_element_type=F32)
        chosen = hit & (order == rank.astype(F32)) & ((lane >> 5) == source)
        table = jnp.where(chosen, 1.0, 0.0).astype(BF16)
        rows = jnp.concatenate([ref[:depth, :] for ref in ins], 0)
        picked = jnp.dot(table, rows, preferred_element_type=F32).astype(BF16)
        for i, out_ref in enumerate(outs):
            out_ref[...] = picked[i * slots : (i + 1) * slots]


def pick_rows(first, second, place):
    width = first[0].shape[1]
    shape = jax.ShapeDtypeStruct((64, width), BF16)
    vmem = pl.BlockSpec(memory_space=pltpu.VMEM)
    out = pl.pallas_call(
        pick_kernel,
        out_shape=[shape] * 16,
        in_specs=[pl.BlockSpec(memory_space=pltpu.SMEM)] + [vmem] * 8,
        out_specs=[vmem] * 16,
        compiler_params=pltpu.CompilerParams(vmem_limit_bytes=16 << 20),
        name="pick_rows",
    )(place, *in_vmem([*first, *second]))
    return out[:8], out[8:]


def load_kernel(*refs):
    *ins, first_sem = refs
    count = len(ins) // 2
    copies = [
        pltpu.make_async_copy(source.at[e], target.at[e], first_sem.at[i, e])
        for i, (source, target) in enumerate(zip(ins[:count], ins[count:]))
        for e in range(source.shape[0])
    ]
    for copy in copies:
        copy.start()
    for copy in copies:
        copy.wait()


def load(*values):
    return pl.pallas_call(
        load_kernel,
        out_shape=[pltpu.VMEM(value.shape, value.dtype) for value in values],
        in_specs=[pl.BlockSpec(memory_space=pl.ANY)] * len(values),
        out_specs=[pl.BlockSpec(memory_space=pltpu.VMEM)] * len(values),
        scratch_shapes=[pltpu.SemaphoreType.DMA((len(values), values[0].shape[0]))],
        compiler_params=pltpu.CompilerParams(vmem_limit_bytes=1 << 20),
        name="load",
    )(*[in_hbm(value) for value in values])


def gate_up_kernel(place, *refs):
    first, second = refs[:8], refs[8:16]
    gate_ref, up_ref, act_ref, sum_ref = refs[16:]
    experts, width, units = gate_ref.shape
    share = first[0].shape[1] // 2
    groups = width // share
    rows = act_ref.shape[1]
    kinds = 2
    half = groups // 2
    for e in range(experts):
        sums = {}
        for back in range(groups):
            source = (first, second)[back // half]
            cut = slice((back % half) * share, (back % half + 1) * share)
            x = jnp.concatenate([ref[e * 32 : (e + 1) * 32, cut] for ref in source], 0)
            depth = lax.rem(place[HEAD] + groups - back, groups) * share
            depth = pl.ds(pl.multiple_of(depth, share), share)
            for kind, ref in enumerate((gate_ref, up_ref)):
                term = jnp.dot(x, ref[e, depth, :], preferred_element_type=F32)
                key = (kind, back // half)
                sums[key] = sums[key] + term if key in sums else term
        for dy in range(4):
            for dc in range(2):
                for dx in range(4):
                    pool = (
                        ((place[ROW] + 4 - dy) & 3) * 8
                        + ((place[COLUMN] + 4 - dx) & 3) * 2
                        + (place[CORE] ^ dc)
                    )
                    a = ((dy * 2 + dc) * 4 + dx) * 8
                    b = ((dx * 2 + dc) * 4 + dy) * 8
                    for kind in range(kinds):
                        sum_ref[kind, pool] = (
                            sums[kind, 0][a : a + 8] + sums[kind, 1][b : b + 8]
                        )
        gate = sum_ref[0].reshape(rows, units)
        up = sum_ref[1].reshape(rows, units)
        act_ref[e] = (gate / (1.0 + jnp.exp(-gate)) * up).astype(act_ref.dtype)


def gate_up(first, second, w_gate, w_up, place, pools, capacity):
    experts, _, units = w_gate.shape
    rows = pools * capacity
    vmem = pl.BlockSpec(memory_space=pltpu.VMEM)
    return pl.pallas_call(
        gate_up_kernel,
        out_shape=jax.ShapeDtypeStruct((experts, rows, units), BF16),
        in_specs=[pl.BlockSpec(memory_space=pltpu.SMEM)] + [vmem] * 18,
        out_specs=vmem,
        scratch_shapes=[pltpu.VMEM((2, pools, capacity, units), F32)],
        compiler_params=pltpu.CompilerParams(vmem_limit_bytes=12 << 20),
        name="gate_up",
    )(place, *in_vmem([*first, *second, w_gate, w_up]))


def down_kernel(*refs):
    *ins, out_ref = refs
    count = len(ins) // 2
    total = 0.0
    for act_ref, weight_ref in zip(ins[:count], ins[count:]):
        total = total + jnp.dot(act_ref[0], weight_ref[0], preferred_element_type=F32)
    out_ref[...] = total.astype(out_ref.dtype).reshape(out_ref.shape)


def down(acts, weights, pools, capacity):
    experts, rows, units = acts[0].shape
    share = weights[0].shape[2]
    return pl.pallas_call(
        down_kernel,
        out_shape=jax.ShapeDtypeStruct((pools, experts * capacity, share), BF16),
        grid=(experts,),
        in_specs=[pl.BlockSpec((1, rows, units), lambda e: (e, 0, 0))] * len(acts)
        + [pl.BlockSpec((1, units, share), lambda e: (e, 0, 0))] * len(weights),
        out_specs=pl.BlockSpec((pools, capacity, share), lambda e: (0, e, 0)),
        compiler_params=pltpu.CompilerParams(
            dimension_semantics=("arbitrary",), vmem_limit_bytes=16 << 20
        ),
        name="down",
    )(*in_vmem([*acts, *weights]))


def route_slots(expert_ids, capacity):
    flat = expert_ids.reshape(-1)
    order = jnp.arange(flat.shape[0])
    earlier = (flat[:, None] == flat[None, :]) & (order[None, :] < order[:, None])
    rank = jnp.sum(earlier.astype(jnp.int32), 1)
    return (flat * capacity + rank).reshape(expert_ids.shape)


def turned(value, step):
    groups = lax.axis_size("head")
    return lax.ppermute(value, "head", [(i, (i + step) % groups) for i in range(groups)])


def moved_in_plane(value, dy, dx, dc):
    pairs = []
    for y in range(4):
        for x in range(4):
            for c in range(2):
                to = (y + dy) % 4 * 8 + (x + dx) % 4 * 2 + (c ^ dc)
                pairs.append((y * 8 + x * 2 + c, to))
    return lax.ppermute(value, "pool", pairs)


def body(
    x_rows,
    query,
    key_cache,
    value_cache,
    new_key,
    new_value,
    lengths,
    out_proj,
    norm_gain,
    expert_ids,
    gate_weights,
    w_gate,
    w_up,
    w_down,
):
    pools = lax.axis_size("pool")
    groups = lax.axis_size("head")
    rows, width = x_rows.shape
    share = width // groups
    experts = w_gate.shape[0]
    capacity = max(2, 2 * expert_ids.shape[0] * expert_ids.shape[1] // (pools * experts))
    slots = experts * capacity
    head = lax.axis_index("head")
    steps = range(1, groups)

    pool = lax.axis_index("pool")
    place = jnp.stack([head, pool >> 3, (pool >> 1) & 3, pool & 1]).astype(jnp.int32)
    own, *away = attend_project(
        query, key_cache, value_cache, new_key, new_value, lengths, place, out_proj, groups
    )
    others = [turned(piece, step) for step, piece in zip(steps, away)]
    slot = route_slots(expert_ids, capacity)
    matching = jnp.arange(pools * slots)[:, None, None] == slot[None, :, :]
    take = jnp.sum(jnp.where(matching, gate_weights[None, :, :], 0.0), 2).T
    take_high = take.astype(BF16)
    take_low = (take - take_high.astype(F32)).astype(BF16)
    ids = jnp.tile(expert_ids.T.astype(BF16), (1, 128 // rows))
    columns = [
        lax.dynamic_slice_in_dim(w_down, lax.rem(head + step, groups) * share, share, 2)
        for step in range(groups)
    ]
    others, columns = lax.optimization_barrier((others, columns))
    hidden = lax.dynamic_slice_in_dim(x_rows, head * share, share, 1).astype(F32) + own
    for other in others:
        hidden = hidden + other.astype(F32)
    slices = [turned(hidden.astype(BF16), step) for step in steps]
    moved = [turned(piece, step) for step, piece in zip(steps, columns[1:])]
    first, second = norm_rows(hidden, slices, norm_gain, ids, place)
    along_x = [first] + [moved_in_plane(first, 0, step, 0) for step in (1, 2, 3)]
    along_y = [second] + [moved_in_plane(second, step, 0, 0) for step in (1, 2, 3)]
    for_y, for_x = pick_rows(along_x, along_y, place)
    ways = [(step, flip) for step in range(4) for flip in range(2)]
    from_y, from_x = list(for_y), list(for_x)
    for step, flip in FAR_ORDER:
        way = ways.index((step, flip))
        from_y[way] = moved_in_plane(for_y[way], step, 0, flip)
        from_x[way] = moved_in_plane(for_x[way], 0, step, flip)
    gate_near, up_near = load(w_gate, w_up)
    act = gate_up(from_y, from_x, gate_near, up_near, place, pools, capacity)
    acts = [act] + [turned(act, step) for step in steps]
    produced = down(acts, [columns[0]] + moved, pools, capacity)
    returned = lax.all_to_all(produced, "pool", split_axis=0, concat_axis=0, tiled=True)
    returned = returned.reshape(pools * slots, share)
    moe = jnp.dot(take_high, returned, preferred_element_type=F32) + jnp.dot(
        take_low, returned, preferred_element_type=F32
    )
    return (hidden + moe).astype(BF16)


def solution(mesh):
    placed = (
        P("pool", None),
        P("pool", "head"),
        P("pool", "head", None, None),
        P("pool", "head", None, None),
        P("pool", "head"),
        P("pool", "head"),
        P("pool"),
        P("head", None),
        P(),
        P("pool", None),
        P("pool", None),
        P("pool", None, "head"),
        P("pool", None, "head"),
        P("pool", "head", None),
    )
    return jax.shard_map(
        body, mesh=mesh, in_specs=placed, out_specs=P("pool", "head"), check_vma=False
    )
```

```python
import jax
import jax.numpy as jnp
from jax import lax
from jax.experimental import pallas as pl
from jax.experimental.pallas import tpu as pltpu
from jax.sharding import PartitionSpec as P


F32 = jnp.float32
BF16 = jnp.bfloat16
GROUP = 8
HEAD, ROW, COLUMN, CORE = range(4)
NEAR_ORDER = (2, 1, 3, 0)
FAR_ORDER = ((2, 0), (2, 1), (1, 0), (3, 0), (1, 1), (3, 1), (0, 1), (0, 0))


def attend_kernel(lengths, place, q_ref, k_ref, v_ref, nk_ref, nv_ref, proj_hbm, *outs):
    *out_refs, rows_ref, proj_ref, sems = outs
    step = pl.program_id(0)
    steps = pl.num_programs(0)
    parts = sems.shape[0]
    depth = proj_ref.shape[0] // parts

    def part(i):
        cut = pl.ds(i * depth, depth)
        return pltpu.make_async_copy(proj_hbm.at[cut], proj_ref.at[cut], sems.at[i])

    @pl.when(step == 0)
    def _():
        for i in range(parts):
            part(i).start()

    size = nk_ref.shape[1]
    heads = q_ref.shape[1] // size
    slots = k_ref.shape[2]
    scale = size ** (-0.5)
    base = pl.multiple_of(step * GROUP, GROUP)
    queries = q_ref[pl.ds(base, GROUP), :].astype(F32)
    new_keys = nk_ref[pl.ds(base, GROUP), :].astype(F32)
    new_values = nv_ref[pl.ds(base, GROUP), :].astype(F32)
    slot_of = lax.broadcasted_iota(jnp.int32, (heads, slots), 1)
    done = []
    blank = jnp.zeros((heads, size), F32)
    for j in range(0, GROUP, 2):
        pair = [
            jnp.concatenate([queries[k : k + 1, i * size : (i + 1) * size] for i in range(heads)], 0)
            for k in (j, j + 1)
        ]
        spread = jnp.concatenate(
            [jnp.concatenate([pair[0], blank], 1), jnp.concatenate([blank, pair[1]], 1)], 0
        )
        keys = jnp.concatenate([k_ref[j, 0], k_ref[j + 1, 0]], 1)
        values = jnp.concatenate([v_ref[j, 0], v_ref[j + 1, 0]], 1)
        scores = (
            lax.dot_general(
                spread.astype(BF16), keys, (((1,), (1,)), ((), ())), preferred_element_type=F32
            )
            * scale
        )
        fresh = [
            jnp.sum(pair[k] * new_keys[j + k : j + k + 1], 1, keepdims=True) for k in range(2)
        ]
        fresh = jnp.concatenate(fresh, 0) * scale
        live = jnp.concatenate([slot_of < lengths[base + j + k] for k in range(2)], 0)
        scores = jnp.where(live, scores, -1e30)
        highest = jnp.maximum(jnp.max(scores, 1, keepdims=True), fresh)
        weights = jnp.where(live, jnp.exp(scores - highest), 0.0)
        own = jnp.exp(fresh - highest)
        total = jnp.sum(weights, 1, keepdims=True) + own
        share = 1.0 / total
        probs = (weights * share).astype(BF16)
        own = (own * share).astype(BF16).astype(F32)
        mixed = jnp.dot(probs, values, preferred_element_type=F32)
        for k in range(2):
            rows = slice(k * heads, (k + 1) * heads)
            part_sum = mixed[rows, k * size : (k + 1) * size] + own[rows] * new_values[j + k : j + k + 1]
            done.append(jnp.concatenate([part_sum[i : i + 1] for i in range(heads)], 1))
    rows_ref[pl.ds(base, GROUP), :] = jnp.concatenate(done, 0)

    @pl.when(step == steps - 1)
    def _():
        attn = rows_ref[...].astype(BF16)
        for i in range(parts):
            part(i).wait()
        groups = len(out_refs)
        share = out_refs[0].shape[1]
        for ahead in [*range(1, groups), 0]:
            column = lax.rem(place[HEAD] + ahead, groups) * share
            weight = proj_ref[:, pl.ds(pl.multiple_of(column, share), share)]
            terms = jnp.dot(attn, weight, preferred_element_type=F32)
            out_refs[ahead][...] = terms.astype(out_refs[ahead].dtype)


def in_hbm(value):
    return pltpu.with_memory_space_constraint(value, pltpu.HBM)


def in_vmem(values):
    return [pltpu.with_memory_space_constraint(value, pltpu.VMEM) for value in values]


def attend_project(query, key_cache, value_cache, new_key, new_value, lengths, place, out_proj, groups):
    rows, wide = query.shape
    size = new_key.shape[1]
    slots = key_cache.shape[2]
    share = out_proj.shape[1] // groups
    whole = lambda shape: pl.BlockSpec(shape, lambda s, *_: (0, 0))
    cache = pl.BlockSpec((GROUP, 1, slots, size), lambda s, *_: (s, 0, 0, 0))
    return pl.pallas_call(
        attend_kernel,
        out_shape=[
            jax.ShapeDtypeStruct((rows, share), BF16 if ahead else F32) for ahead in range(groups)
        ],
        grid_spec=pltpu.PrefetchScalarGridSpec(
            num_scalar_prefetch=2,
            grid=(rows // GROUP,),
            in_specs=[
                whole((rows, wide)),
                cache,
                cache,
                whole((rows, size)),
                whole((rows, size)),
                pl.BlockSpec(memory_space=pl.ANY),
            ],
            out_specs=[whole((rows, share))] * groups,
            scratch_shapes=[
                pltpu.VMEM((rows, wide), F32),
                pltpu.VMEM(out_proj.shape, BF16),
                pltpu.SemaphoreType.DMA((4,)),
            ],
        ),
        compiler_params=pltpu.CompilerParams(
            dimension_semantics=("arbitrary",), vmem_limit_bytes=24 << 20
        ),
        name="attend_project",
    )(
        in_hbm(lengths),
        place,
        in_hbm(query),
        in_hbm(key_cache),
        in_hbm(value_cache),
        in_hbm(new_key),
        in_hbm(new_value),
        in_hbm(out_proj),
    )


def norm_kernel(place, own_ref, *refs):
    *other_refs, gain_ref, ids_ref, first_ref, second_ref = refs
    groups = 1 + len(other_refs)
    rows, share = own_ref.shape
    blocks = [own_ref[...]] + [ref[...].astype(F32) for ref in other_refs]
    square = sum(jnp.sum(block * block, 1, keepdims=True) for block in blocks)
    inverse = lax.rsqrt(square / (groups * share) + 1e-06)
    half = groups // 2
    for back, block in enumerate(blocks):
        gain = gain_ref[lax.rem(place[HEAD] + groups - back, groups)]
        out_ref = (first_ref, second_ref)[back // half]
        cut = (back % half) * share
        out_ref[:rows, cut : cut + share] = (block * inverse * gain).astype(BF16)
    for out_ref in (first_ref, second_ref):
        out_ref[rows:, :] = jnp.zeros((ids_ref.shape[0], half * share), BF16)
        out_ref[rows:, : ids_ref.shape[1]] = ids_ref[...]


def norm_rows(own, others, norm_gain, ids, place):
    rows, share = own.shape
    groups = 1 + len(others)
    gains = norm_gain.reshape(groups, 1, share)
    shape = jax.ShapeDtypeStruct((rows + ids.shape[0], groups // 2 * share), BF16)
    vmem = pl.BlockSpec(memory_space=pltpu.VMEM)
    return pl.pallas_call(
        norm_kernel,
        out_shape=[shape, shape],
        in_specs=[pl.BlockSpec(memory_space=pltpu.SMEM)] + [vmem] * (groups + 2),
        out_specs=[vmem, vmem],
        compiler_params=pltpu.CompilerParams(vmem_limit_bytes=8 << 20),
        name="norm_rows",
    )(place, *in_vmem([own, *others]), gains, ids)


def pick_kernel(place, *refs):
    count = 4
    pools = (place[ROW], place[COLUMN], place[CORE])
    slots, near, cores = refs[-1].shape[0], count, 2
    targets = count * cores
    depth = 32
    lanes = near * depth
    total = targets * slots
    line = lax.broadcasted_iota(jnp.int32, (total, lanes), 0)
    lane = lax.broadcasted_iota(jnp.int32, (total, lanes), 1)
    step, flip = line >> 7, (line >> 6) & 1
    expert, source, rank = (line >> 5) & 1, (line >> 3) & 3, line & 7
    core = pools[2] ^ flip
    upper_line = lax.broadcasted_iota(jnp.int32, (lanes, lanes), 0)
    upper_lane = lax.broadcasted_iota(jnp.int32, (lanes, lanes), 1)
    earlier = ((upper_line < upper_lane) & ((upper_line >> 5) == (upper_lane >> 5))).astype(F32)
    id_lane = lax.broadcasted_iota(jnp.int32, (8, lanes), 1) >> 5
    for half in range(2):
        ins = [refs[2 * NEAR_ORDER.index(back) + half] for back in range(near)]
        outs = refs[(2 + 2 * half) * near : (4 + 2 * half) * near]
        if half == 0:
            target = ((pools[0] + step) & 3) * 8 + pools[1] * 2 + core
        else:
            target = pools[0] * 8 + ((pools[1] + step) & 3) * 2 + core
        wanted = (target * 2 + expert).astype(F32)
        ids = jnp.zeros((8, lanes), F32)
        for back, ref in enumerate(ins):
            ids = jnp.where(id_lane == back, ref[depth:, :lanes].astype(F32), ids)
        hit = ids[0:1] == wanted
        for k in range(1, 8):
            hit = hit | (ids[k : k + 1] == wanted)
        hits = jnp.where(hit, 1.0, 0.0).astype(BF16)
        order = jnp.dot(hits, earlier.astype(BF16), preferred_element_type=F32)
        chosen = hit & (order == rank.astype(F32)) & ((lane >> 5) == source)
        table = jnp.where(chosen, 1.0, 0.0).astype(BF16)
        rows = jnp.concatenate([ref[:depth, :] for ref in ins], 0)
        picked = jnp.dot(table, rows, preferred_element_type=F32).astype(BF16)
        for i, out_ref in enumerate(outs):
            out_ref[...] = picked[i * slots : (i + 1) * slots]


def pick_rows(first, second, place):
    width = first[0].shape[1]
    shape = jax.ShapeDtypeStruct((64, width), BF16)
    vmem = pl.BlockSpec(memory_space=pltpu.VMEM)
    out = pl.pallas_call(
        pick_kernel,
        out_shape=[shape] * 16,
        in_specs=[pl.BlockSpec(memory_space=pltpu.SMEM)] + [vmem] * 8,
        out_specs=[vmem] * 16,
        compiler_params=pltpu.CompilerParams(vmem_limit_bytes=16 << 20),
        name="pick_rows",
    )(place, *in_vmem([part[back] for back in NEAR_ORDER for part in (first, second)]))
    return out[:8], out[8:]


def load_kernel(*refs):
    *ins, first_sem = refs
    count = len(ins) // 2
    copies = [
        pltpu.make_async_copy(source.at[e], target.at[e], first_sem.at[i, e])
        for i, (source, target) in enumerate(zip(ins[:count], ins[count:]))
        for e in range(source.shape[0])
    ]
    for copy in copies:
        copy.start()
    for copy in copies:
        copy.wait()


def load(*values):
    return pl.pallas_call(
        load_kernel,
        out_shape=[pltpu.VMEM(value.shape, value.dtype) for value in values],
        in_specs=[pl.BlockSpec(memory_space=pl.ANY)] * len(values),
        out_specs=[pl.BlockSpec(memory_space=pltpu.VMEM)] * len(values),
        scratch_shapes=[pltpu.SemaphoreType.DMA((len(values), values[0].shape[0]))],
        compiler_params=pltpu.CompilerParams(vmem_limit_bytes=1 << 20),
        name="load",
    )(*[in_hbm(value) for value in values])


def gate_up_kernel(place, *refs):
    first, second = [None] * 8, [None] * 8
    for i, (step, flip) in enumerate(FAR_ORDER):
        first[step * 2 + flip], second[step * 2 + flip] = refs[2 * i : 2 * i + 2]
    gate_ref, up_ref, act_ref, sum_ref = refs[16:]
    experts, width, units = gate_ref.shape
    share = first[0].shape[1] // 2
    groups = width // share
    rows = act_ref.shape[1]
    kinds = 2
    half = groups // 2
    for e in range(experts):
        sums = {}
        for back in range(groups):
            source = (first, second)[back // half]
            cut = slice((back % half) * share, (back % half + 1) * share)
            x = jnp.concatenate([ref[e * 32 : (e + 1) * 32, cut] for ref in source], 0)
            depth = lax.rem(place[HEAD] + groups - back, groups) * share
            depth = pl.ds(pl.multiple_of(depth, share), share)
            for kind, ref in enumerate((gate_ref, up_ref)):
                term = jnp.dot(x, ref[e, depth, :], preferred_element_type=F32)
                key = (kind, back // half)
                sums[key] = sums[key] + term if key in sums else term
        for dy in range(4):
            for dc in range(2):
                for dx in range(4):
                    pool = (
                        ((place[ROW] + 4 - dy) & 3) * 8
                        + ((place[COLUMN] + 4 - dx) & 3) * 2
                        + (place[CORE] ^ dc)
                    )
                    a = ((dy * 2 + dc) * 4 + dx) * 8
                    b = ((dx * 2 + dc) * 4 + dy) * 8
                    for kind in range(kinds):
                        sum_ref[kind, pool] = (
                            sums[kind, 0][a : a + 8] + sums[kind, 1][b : b + 8]
                        )
        gate = sum_ref[0].reshape(rows, units)
        up = sum_ref[1].reshape(rows, units)
        act_ref[e] = (gate / (1.0 + jnp.exp(-gate)) * up).astype(act_ref.dtype)


def gate_up(first, second, w_gate, w_up, place, pools, capacity):
    experts, _, units = w_gate.shape
    rows = pools * capacity
    vmem = pl.BlockSpec(memory_space=pltpu.VMEM)
    return pl.pallas_call(
        gate_up_kernel,
        out_shape=jax.ShapeDtypeStruct((experts, rows, units), BF16),
        in_specs=[pl.BlockSpec(memory_space=pltpu.SMEM)] + [vmem] * 18,
        out_specs=vmem,
        scratch_shapes=[pltpu.VMEM((2, pools, capacity, units), F32)],
        compiler_params=pltpu.CompilerParams(vmem_limit_bytes=12 << 20),
        name="gate_up",
    )(place, *in_vmem([part[step * 2 + flip] for step, flip in FAR_ORDER for part in (first, second)]), *in_vmem([w_gate, w_up]))


def down_kernel(*refs):
    *ins, out_ref = refs
    count = len(ins) // 2
    total = 0.0
    for act_ref, weight_ref in zip(ins[:count], ins[count:]):
        total = total + jnp.dot(act_ref[0], weight_ref[0], preferred_element_type=F32)
    out_ref[...] = total.astype(out_ref.dtype).reshape(out_ref.shape)


def down(acts, weights, pools, capacity):
    experts, rows, units = acts[0].shape
    share = weights[0].shape[2]
    return pl.pallas_call(
        down_kernel,
        out_shape=jax.ShapeDtypeStruct((pools, experts * capacity, share), BF16),
        grid=(experts,),
        in_specs=[pl.BlockSpec((1, rows, units), lambda e: (e, 0, 0))] * len(acts)
        + [pl.BlockSpec((1, units, share), lambda e: (e, 0, 0))] * len(weights),
        out_specs=pl.BlockSpec((pools, capacity, share), lambda e: (0, e, 0)),
        compiler_params=pltpu.CompilerParams(
            dimension_semantics=("arbitrary",), vmem_limit_bytes=16 << 20
        ),
        name="down",
    )(*in_vmem([*acts, *weights]))


def route_slots(expert_ids, capacity):
    flat = expert_ids.reshape(-1)
    order = jnp.arange(flat.shape[0])
    earlier = (flat[:, None] == flat[None, :]) & (order[None, :] < order[:, None])
    rank = jnp.sum(earlier.astype(jnp.int32), 1)
    return (flat * capacity + rank).reshape(expert_ids.shape)


def turned(value, step):
    groups = lax.axis_size("head")
    return lax.ppermute(value, "head", [(i, (i + step) % groups) for i in range(groups)])


def moved_in_plane(value, dy, dx, dc):
    pairs = []
    for y in range(4):
        for x in range(4):
            for c in range(2):
                to = (y + dy) % 4 * 8 + (x + dx) % 4 * 2 + (c ^ dc)
                pairs.append((y * 8 + x * 2 + c, to))
    return lax.ppermute(value, "pool", pairs)


def body(
    x_rows,
    query,
    key_cache,
    value_cache,
    new_key,
    new_value,
    lengths,
    out_proj,
    norm_gain,
    expert_ids,
    gate_weights,
    w_gate,
    w_up,
    w_down,
):
    pools = lax.axis_size("pool")
    groups = lax.axis_size("head")
    rows, width = x_rows.shape
    share = width // groups
    experts = w_gate.shape[0]
    capacity = max(2, 2 * expert_ids.shape[0] * expert_ids.shape[1] // (pools * experts))
    slots = experts * capacity
    head = lax.axis_index("head")
    steps = range(1, groups)

    pool = lax.axis_index("pool")
    place = jnp.stack([head, pool >> 3, (pool >> 1) & 3, pool & 1]).astype(jnp.int32)
    own, *away = attend_project(
        query, key_cache, value_cache, new_key, new_value, lengths, place, out_proj, groups
    )
    others = [turned(piece, step) for step, piece in zip(steps, away)]
    slot = route_slots(expert_ids, capacity)
    matching = jnp.arange(pools * slots)[:, None, None] == slot[None, :, :]
    take = jnp.sum(jnp.where(matching, gate_weights[None, :, :], 0.0), 2).T
    take_high = take.astype(BF16)
    take_low = (take - take_high.astype(F32)).astype(BF16)
    ids = jnp.tile(expert_ids.T.astype(BF16), (1, 128 // rows))
    columns = [
        lax.dynamic_slice_in_dim(w_down, lax.rem(head + step, groups) * share, share, 2)
        for step in range(groups)
    ]
    others, columns = lax.optimization_barrier((others, columns))
    hidden = lax.dynamic_slice_in_dim(x_rows, head * share, share, 1).astype(F32) + own
    for other in others:
        hidden = hidden + other.astype(F32)
    slices = [turned(hidden.astype(BF16), step) for step in steps]
    moved = [turned(piece, step) for step, piece in zip(steps, columns[1:])]
    first, second = norm_rows(hidden, slices, norm_gain, ids, place)
    along_x = [first] + [moved_in_plane(first, 0, step, 0) for step in (1, 2, 3)]
    along_y = [second] + [moved_in_plane(second, step, 0, 0) for step in (1, 2, 3)]
    for_y, for_x = pick_rows(along_x, along_y, place)
    ways = [(step, flip) for step in range(4) for flip in range(2)]
    from_y, from_x = list(for_y), list(for_x)
    for step, flip in FAR_ORDER[:-1]:
        way = ways.index((step, flip))
        from_y[way] = moved_in_plane(for_y[way], step, 0, flip)
        from_x[way] = moved_in_plane(for_x[way], 0, step, flip)
    gate_near, up_near = load(w_gate, w_up)
    act = gate_up(from_y, from_x, gate_near, up_near, place, pools, capacity)
    acts = [act] + [turned(act, step) for step in steps]
    produced = down(acts, [columns[0]] + moved, pools, capacity)
    returned = lax.all_to_all(produced, "pool", split_axis=0, concat_axis=0, tiled=True)
    returned = returned.reshape(pools * slots, share)
    moe = jnp.dot(take_high, returned, preferred_element_type=F32) + jnp.dot(
        take_low, returned, preferred_element_type=F32
    )
    return (hidden + moe).astype(BF16)


def solution(mesh):
    placed = (
        P("pool", None),
        P("pool", "head"),
        P("pool", "head", None, None),
        P("pool", "head", None, None),
        P("pool", "head"),
        P("pool", "head"),
        P("pool"),
        P("head", None),
        P(),
        P("pool", None),
        P("pool", None),
        P("pool", None, "head"),
        P("pool", None, "head"),
        P("pool", "head", None),
    )
    return jax.shard_map(body, mesh=mesh, in_specs=placed, out_specs=P("pool", "head"), check_vma=False)
```

```python
import jax
import jax.numpy as jnp
from jax import lax
from jax.experimental import pallas as pl
from jax.experimental.pallas import tpu as pltpu
from jax.sharding import PartitionSpec as P


F32 = jnp.float32
BF16 = jnp.bfloat16
GROUP = 8
HEAD, ROW, COLUMN, CORE = range(4)
NEAR_ORDER = (2, 1, 3, 0)
FAR_ORDER = ((2, 0), (2, 1), (1, 0), (3, 0), (1, 1), (3, 1), (0, 1), (0, 0))


def attend_kernel(lengths, place, q_ref, k_hbm, v_hbm, nk_ref, nv_ref, proj_hbm, *outs):
    *out_refs, k_ref, v_ref, rows_ref, proj_ref, sum_ref, cache_sems, proj_sems = outs
    steps, parts = cache_sems.shape[1], proj_sems.shape[0]
    depth = proj_ref.shape[0] // parts

    def cached(g, kind):
        cut = pl.ds(g * GROUP, GROUP)
        source, target = ((k_hbm, k_ref), (v_hbm, v_ref))[kind]
        return pltpu.make_async_copy(source.at[cut, 0], target.at[cut], cache_sems.at[kind, g])

    def part(i):
        cut = pl.ds(i * depth, depth)
        return pltpu.make_async_copy(proj_hbm.at[cut], proj_ref.at[cut], proj_sems.at[i])

    for g in range(steps):
        for kind in range(2):
            cached(g, kind).start()
    for g in range(steps):
        for kind in range(2):
            cached(g, kind).wait()
        part(g).start()
        attend_group(g * GROUP, lengths, q_ref, k_ref, v_ref, nk_ref, nv_ref, rows_ref)
    attn = rows_ref[...].astype(BF16)
    groups = len(out_refs)
    share = out_refs[0].shape[1]
    for i in range(parts):
        part(i).wait()
        cut = slice(i * depth, (i + 1) * depth)
        for ahead in range(groups):
            column = lax.rem(place[HEAD] + ahead, groups) * share
            weight = proj_ref[cut, pl.ds(pl.multiple_of(column, share), share)]
            terms = jnp.dot(attn[:, cut], weight, preferred_element_type=F32)
            if i:
                terms = terms + sum_ref[ahead]
            if i < parts - 1:
                sum_ref[ahead] = terms
            else:
                out_refs[ahead][...] = terms.astype(out_refs[ahead].dtype)


def attend_group(base, lengths, q_ref, k_ref, v_ref, nk_ref, nv_ref, rows_ref):
    size = nk_ref.shape[1]
    heads = q_ref.shape[1] // size
    slots = k_ref.shape[1]
    scale = size ** (-0.5)
    queries = q_ref[pl.ds(base, GROUP), :].astype(F32)
    new_keys = nk_ref[pl.ds(base, GROUP), :].astype(F32)
    new_values = nv_ref[pl.ds(base, GROUP), :].astype(F32)
    slot_of = lax.broadcasted_iota(jnp.int32, (heads, slots), 1)
    blank = jnp.zeros((heads, size), F32)
    split = [
        jnp.concatenate([queries[j : j + 1, i * size : (i + 1) * size] for i in range(heads)], 0)
        for j in range(GROUP)
    ]
    scores = []
    for j in range(0, GROUP, 2):
        spread = jnp.concatenate(
            [jnp.concatenate([split[j], blank], 1), jnp.concatenate([blank, split[j + 1]], 1)], 0
        )
        keys = jnp.concatenate([k_ref[base + j], k_ref[base + j + 1]], 1)
        scores.append(
            lax.dot_general(
                spread.astype(BF16), keys, (((1,), (1,)), ((), ())), preferred_element_type=F32
            )
        )
    scores = jnp.concatenate(scores, 0) * scale
    new_keys, new_values = (
        jnp.concatenate([jnp.broadcast_to(new[j : j + 1], (heads, size)) for j in range(GROUP)], 0)
        for new in (new_keys, new_values)
    )
    fresh = jnp.sum(jnp.concatenate(split, 0) * new_keys, 1, keepdims=True) * scale
    live = jnp.concatenate([slot_of < lengths[base + j] for j in range(GROUP)], 0)
    scores = jnp.where(live, scores, -1e30)
    highest = jnp.maximum(jnp.max(scores, 1, keepdims=True), fresh)
    weights = jnp.where(live, jnp.exp(scores - highest), 0.0)
    own = jnp.exp(fresh - highest)
    total = jnp.sum(weights, 1, keepdims=True) + own
    share = 1.0 / total
    probs = (weights * share).astype(BF16)
    own = (own * share).astype(BF16).astype(F32) * new_values
    mixed = []
    for j in range(0, GROUP, 2):
        values = jnp.concatenate([v_ref[base + j], v_ref[base + j + 1]], 1)
        rows = slice(j * heads, (j + 2) * heads)
        pair = jnp.dot(probs[rows], values, preferred_element_type=F32)
        mixed += [pair[:heads, :size], pair[heads:, size:]]
    done = []
    for j in range(GROUP):
        mix = mixed[j] + own[j * heads : (j + 1) * heads]
        done.append(jnp.concatenate([mix[i : i + 1] for i in range(heads)], 1))
    rows_ref[pl.ds(base, GROUP), :] = jnp.concatenate(done, 0)


def in_hbm(value):
    return pltpu.with_memory_space_constraint(value, pltpu.HBM)


def in_vmem(values):
    return [pltpu.with_memory_space_constraint(value, pltpu.VMEM) for value in values]


def attend_project(query, key_cache, value_cache, new_key, new_value, lengths, place, out_proj, groups):
    rows, wide = query.shape
    size = new_key.shape[1]
    slots = key_cache.shape[2]
    share = out_proj.shape[1] // groups
    vmem = pl.BlockSpec(memory_space=pltpu.VMEM)
    smem = pl.BlockSpec(memory_space=pltpu.SMEM)
    hbm = pl.BlockSpec(memory_space=pl.ANY)
    return pl.pallas_call(
        attend_kernel,
        out_shape=[
            jax.ShapeDtypeStruct((rows, share), BF16 if ahead else F32) for ahead in range(groups)
        ],
        in_specs=[smem, smem, vmem, hbm, hbm, vmem, vmem, hbm],
        out_specs=[vmem] * groups,
        scratch_shapes=[
            pltpu.VMEM((rows, slots, size), BF16),
            pltpu.VMEM((rows, slots, size), BF16),
            pltpu.VMEM((rows, wide), F32),
            pltpu.VMEM(out_proj.shape, BF16),
            pltpu.VMEM((groups, rows, share), F32),
            pltpu.SemaphoreType.DMA((2, rows // GROUP)),
            pltpu.SemaphoreType.DMA((rows // GROUP,)),
        ],
        compiler_params=pltpu.CompilerParams(vmem_limit_bytes=24 << 20),
        name="attend_project",
    )(
        in_hbm(lengths),
        place,
        in_hbm(query),
        in_hbm(key_cache),
        in_hbm(value_cache),
        in_hbm(new_key),
        in_hbm(new_value),
        in_hbm(out_proj),
    )


def norm_kernel(place, own_ref, *refs):
    *other_refs, gain_ref, ids_ref, first_ref, second_ref = refs
    groups = 1 + len(other_refs)
    rows, share = own_ref.shape
    blocks = [own_ref[...]] + [ref[...].astype(F32) for ref in other_refs]
    square = sum(jnp.sum(block * block, 1, keepdims=True) for block in blocks)
    inverse = lax.rsqrt(square / (groups * share) + 1e-06)
    half = groups // 2
    for back, block in enumerate(blocks):
        gain = gain_ref[lax.rem(place[HEAD] + groups - back, groups)]
        out_ref = (first_ref, second_ref)[back // half]
        cut = (back % half) * share
        out_ref[:rows, cut : cut + share] = (block * inverse * gain).astype(BF16)
    for out_ref in (first_ref, second_ref):
        out_ref[rows:, :] = jnp.zeros((ids_ref.shape[0], half * share), BF16)
        out_ref[rows:, : ids_ref.shape[1]] = ids_ref[...]


def norm_rows(own, others, norm_gain, ids, place):
    rows, share = own.shape
    groups = 1 + len(others)
    gains = norm_gain.reshape(groups, 1, share)
    shape = jax.ShapeDtypeStruct((rows + ids.shape[0], groups // 2 * share), BF16)
    vmem = pl.BlockSpec(memory_space=pltpu.VMEM)
    return pl.pallas_call(
        norm_kernel,
        out_shape=[shape, shape],
        in_specs=[pl.BlockSpec(memory_space=pltpu.SMEM)] + [vmem] * (groups + 2),
        out_specs=[vmem, vmem],
        compiler_params=pltpu.CompilerParams(vmem_limit_bytes=8 << 20),
        name="norm_rows",
    )(place, *in_vmem([own, *others]), gains, ids)


def pick_kernel(place, *refs):
    count = 4
    pools = (place[ROW], place[COLUMN], place[CORE])
    slots, near, cores = refs[-1].shape[0], count, 2
    targets = count * cores
    depth = 32
    lanes = near * depth
    total = targets * slots
    line = lax.broadcasted_iota(jnp.int32, (total, lanes), 0)
    lane = lax.broadcasted_iota(jnp.int32, (total, lanes), 1)
    step, flip = line >> 7, (line >> 6) & 1
    expert, source, rank = (line >> 5) & 1, (line >> 3) & 3, line & 7
    core = pools[2] ^ flip
    upper_line = lax.broadcasted_iota(jnp.int32, (lanes, lanes), 0)
    upper_lane = lax.broadcasted_iota(jnp.int32, (lanes, lanes), 1)
    earlier = ((upper_line < upper_lane) & ((upper_line >> 5) == (upper_lane >> 5))).astype(F32)
    id_lane = lax.broadcasted_iota(jnp.int32, (8, lanes), 1) >> 5
    for half in range(2):
        ins = [refs[2 * NEAR_ORDER.index(back) + half] for back in range(near)]
        outs = refs[(2 + 2 * half) * near : (4 + 2 * half) * near]
        if half == 0:
            target = ((pools[0] + step) & 3) * 8 + pools[1] * 2 + core
        else:
            target = pools[0] * 8 + ((pools[1] + step) & 3) * 2 + core
        wanted = (target * 2 + expert).astype(F32)
        ids = jnp.zeros((8, lanes), F32)
        for back, ref in enumerate(ins):
            ids = jnp.where(id_lane == back, ref[depth:, :lanes].astype(F32), ids)
        hit = ids[0:1] == wanted
        for k in range(1, 8):
            hit = hit | (ids[k : k + 1] == wanted)
        hits = jnp.where(hit, 1.0, 0.0).astype(BF16)
        order = jnp.dot(hits, earlier.astype(BF16), preferred_element_type=F32)
        chosen = hit & (order == rank.astype(F32)) & ((lane >> 5) == source)
        table = jnp.where(chosen, 1.0, 0.0).astype(BF16)
        rows = jnp.concatenate([ref[:depth, :] for ref in ins], 0)
        picked = jnp.dot(table, rows, preferred_element_type=F32).astype(BF16)
        for i, out_ref in enumerate(outs):
            out_ref[...] = picked[i * slots : (i + 1) * slots]


def pick_rows(first, second, place):
    width = first[0].shape[1]
    shape = jax.ShapeDtypeStruct((64, width), BF16)
    vmem = pl.BlockSpec(memory_space=pltpu.VMEM)
    out = pl.pallas_call(
        pick_kernel,
        out_shape=[shape] * 16,
        in_specs=[pl.BlockSpec(memory_space=pltpu.SMEM)] + [vmem] * 8,
        out_specs=[vmem] * 16,
        compiler_params=pltpu.CompilerParams(vmem_limit_bytes=16 << 20),
        name="pick_rows",
    )(place, *in_vmem([part[back] for back in NEAR_ORDER for part in (first, second)]))
    return out[:8], out[8:]


def load_kernel(*refs):
    *ins, first_sem = refs
    count = len(ins) // 2
    copies = [
        pltpu.make_async_copy(source.at[e], target.at[e], first_sem.at[i, e])
        for i, (source, target) in enumerate(zip(ins[:count], ins[count:]))
        for e in range(source.shape[0])
    ]
    for copy in copies:
        copy.start()
    for copy in copies:
        copy.wait()


def load(*values):
    return pl.pallas_call(
        load_kernel,
        out_shape=[pltpu.VMEM(value.shape, value.dtype) for value in values],
        in_specs=[pl.BlockSpec(memory_space=pl.ANY)] * len(values),
        out_specs=[pl.BlockSpec(memory_space=pltpu.VMEM)] * len(values),
        scratch_shapes=[pltpu.SemaphoreType.DMA((len(values), values[0].shape[0]))],
        compiler_params=pltpu.CompilerParams(vmem_limit_bytes=1 << 20),
        name="load",
    )(*[in_hbm(value) for value in values])


def cut_kernel(place, source, *refs):
    *targets, sems = refs
    groups = len(targets) + 1
    share = targets[0].shape[2]
    copies = []
    for ahead, target in enumerate(targets, 1):
        column = pl.multiple_of(lax.rem(place[HEAD] + ahead, groups) * share, share)
        copies.append(
            pltpu.make_async_copy(source.at[:, :, pl.ds(column, share)], target, sems.at[ahead - 1])
        )
    for copy in copies:
        copy.start()
    for copy in copies:
        copy.wait()


def cut_columns(value, place, groups):
    experts, depth, width = value.shape
    shape = (experts, depth, width // groups)
    return pl.pallas_call(
        cut_kernel,
        out_shape=[pltpu.VMEM(shape, value.dtype)] * (groups - 1),
        in_specs=[pl.BlockSpec(memory_space=pltpu.SMEM), pl.BlockSpec(memory_space=pl.ANY)],
        out_specs=[pl.BlockSpec(memory_space=pltpu.VMEM)] * (groups - 1),
        scratch_shapes=[pltpu.SemaphoreType.DMA((groups - 1,))],
        compiler_params=pltpu.CompilerParams(vmem_limit_bytes=8 << 20),
        name="cut_columns",
    )(place, in_hbm(value))


def gate_up_kernel(place, *refs):
    first, second = [None] * 8, [None] * 8
    for i, (step, flip) in enumerate(FAR_ORDER):
        first[step * 2 + flip], second[step * 2 + flip] = refs[2 * i : 2 * i + 2]
    gate_ref, up_ref, act_ref, sum_ref = refs[16:]
    experts, width, units = gate_ref.shape
    share = first[0].shape[1] // 2
    groups = width // share
    rows = act_ref.shape[1]
    kinds = 2
    half = groups // 2
    for e in range(experts):
        sums = {}
        for back in range(groups):
            source = (first, second)[back // half]
            cut = slice((back % half) * share, (back % half + 1) * share)
            x = jnp.concatenate([ref[e * 32 : (e + 1) * 32, cut] for ref in source], 0)
            depth = lax.rem(place[HEAD] + groups - back, groups) * share
            depth = pl.ds(pl.multiple_of(depth, share), share)
            for kind, ref in enumerate((gate_ref, up_ref)):
                term = jnp.dot(x, ref[e, depth, :], preferred_element_type=F32)
                key = (kind, back // half)
                sums[key] = sums[key] + term if key in sums else term
        for dy in range(4):
            for dc in range(2):
                for dx in range(4):
                    pool = (
                        ((place[ROW] + 4 - dy) & 3) * 8
                        + ((place[COLUMN] + 4 - dx) & 3) * 2
                        + (place[CORE] ^ dc)
                    )
                    a = ((dy * 2 + dc) * 4 + dx) * 8
                    b = ((dx * 2 + dc) * 4 + dy) * 8
                    for kind in range(kinds):
                        sum_ref[kind, pool] = (
                            sums[kind, 0][a : a + 8] + sums[kind, 1][b : b + 8]
                        )
        gate = sum_ref[0].reshape(rows, units)
        up = sum_ref[1].reshape(rows, units)
        act_ref[e] = (gate / (1.0 + jnp.exp(-gate)) * up).astype(act_ref.dtype)


def gate_up(first, second, w_gate, w_up, place, pools, capacity):
    experts, _, units = w_gate.shape
    rows = pools * capacity
    vmem = pl.BlockSpec(memory_space=pltpu.VMEM)
    return pl.pallas_call(
        gate_up_kernel,
        out_shape=jax.ShapeDtypeStruct((experts, rows, units), BF16),
        in_specs=[pl.BlockSpec(memory_space=pltpu.SMEM)] + [vmem] * 18,
        out_specs=vmem,
        scratch_shapes=[pltpu.VMEM((2, pools, capacity, units), F32)],
        compiler_params=pltpu.CompilerParams(vmem_limit_bytes=12 << 20),
        name="gate_up",
    )(place, *in_vmem([part[step * 2 + flip] for step, flip in FAR_ORDER for part in (first, second)]), *in_vmem([w_gate, w_up]))


def down_kernel(place, *refs):
    *ins, out_ref = refs
    count = len(ins) // 2
    total = 0.0
    for act_ref, weight_ref in zip(ins[:count], ins[count:]):
        total = total + jnp.dot(act_ref[0], weight_ref[0], preferred_element_type=F32)
    out_ref[...] = total.astype(out_ref.dtype).reshape(out_ref.shape)


def down(acts, w_down, moved, place, pools, capacity):
    experts, rows, units = acts[0].shape
    share = moved[0].shape[2]
    return pl.pallas_call(
        down_kernel,
        out_shape=jax.ShapeDtypeStruct((pools, experts * capacity, share), BF16),
        grid_spec=pltpu.PrefetchScalarGridSpec(
            num_scalar_prefetch=1,
            grid=(experts,),
            in_specs=[pl.BlockSpec((1, rows, units), lambda e, p: (e, 0, 0))] * len(acts)
            + [pl.BlockSpec((1, units, share), lambda e, p: (e, 0, p[HEAD]))]
            + [pl.BlockSpec((1, units, share), lambda e, p: (e, 0, 0))] * len(moved),
            out_specs=pl.BlockSpec((pools, capacity, share), lambda e, p: (0, e, 0)),
        ),
        compiler_params=pltpu.CompilerParams(
            dimension_semantics=("arbitrary",), vmem_limit_bytes=16 << 20
        ),
        name="down",
    )(place, *in_vmem(acts), in_hbm(w_down), *in_vmem(moved))


def route_slots(expert_ids, capacity):
    flat = expert_ids.reshape(-1)
    order = jnp.arange(flat.shape[0])
    earlier = (flat[:, None] == flat[None, :]) & (order[None, :] < order[:, None])
    rank = jnp.sum(earlier.astype(jnp.int32), 1)
    return (flat * capacity + rank).reshape(expert_ids.shape)


def turned(value, step):
    groups = lax.axis_size("head")
    return lax.ppermute(value, "head", [(i, (i + step) % groups) for i in range(groups)])


def moved_in_plane(value, dy, dx, dc):
    pairs = []
    for y in range(4):
        for x in range(4):
            for c in range(2):
                to = (y + dy) % 4 * 8 + (x + dx) % 4 * 2 + (c ^ dc)
                pairs.append((y * 8 + x * 2 + c, to))
    return lax.ppermute(value, "pool", pairs)


def body(
    x_rows,
    query,
    key_cache,
    value_cache,
    new_key,
    new_value,
    lengths,
    out_proj,
    norm_gain,
    expert_ids,
    gate_weights,
    w_gate,
    w_up,
    w_down,
):
    pools = lax.axis_size("pool")
    groups = lax.axis_size("head")
    rows, width = x_rows.shape
    share = width // groups
    experts = w_gate.shape[0]
    capacity = max(2, 2 * expert_ids.shape[0] * expert_ids.shape[1] // (pools * experts))
    slots = experts * capacity
    head = lax.axis_index("head")
    steps = range(1, groups)

    pool = lax.axis_index("pool")
    place = jnp.stack([head, pool >> 3, (pool >> 1) & 3, pool & 1]).astype(jnp.int32)
    own, *away = attend_project(
        query, key_cache, value_cache, new_key, new_value, lengths, place, out_proj, groups
    )
    others = [turned(piece, step) for step, piece in zip(steps, away)]
    slot = route_slots(expert_ids, capacity)
    matching = jnp.arange(pools * slots)[:, None, None] == slot[None, :, :]
    take = jnp.sum(jnp.where(matching, gate_weights[None, :, :], 0.0), 2).T
    take_high = take.astype(BF16)
    take_low = (take - take_high.astype(F32)).astype(BF16)
    ids = jnp.tile(expert_ids.T.astype(BF16), (1, 128 // rows))
    columns = cut_columns(w_down, place, groups)
    others, columns = lax.optimization_barrier((others, columns))
    hidden = lax.dynamic_slice_in_dim(x_rows, head * share, share, 1).astype(F32) + own
    for other in others:
        hidden = hidden + other.astype(F32)
    slices = [turned(hidden.astype(BF16), step) for step in steps]
    moved = [turned(piece, step) for step, piece in zip(steps, columns)]
    first, second = norm_rows(hidden, slices, norm_gain, ids, place)
    along_x = [first] + [moved_in_plane(first, 0, step, 0) for step in (1, 2, 3)]
    along_y = [second] + [moved_in_plane(second, step, 0, 0) for step in (1, 2, 3)]
    for_y, for_x = pick_rows(along_x, along_y, place)
    ways = [(step, flip) for step in range(4) for flip in range(2)]
    from_y, from_x = list(for_y), list(for_x)
    for step, flip in FAR_ORDER[:-1]:
        way = ways.index((step, flip))
        from_y[way] = moved_in_plane(for_y[way], step, 0, flip)
        from_x[way] = moved_in_plane(for_x[way], 0, step, flip)
    gate_near, up_near = load(w_gate, w_up)
    act = gate_up(from_y, from_x, gate_near, up_near, place, pools, capacity)
    acts = [act] + [turned(act, step) for step in steps]
    produced = down(acts, w_down, moved, place, pools, capacity)
    returned = lax.all_to_all(produced, "pool", split_axis=0, concat_axis=0, tiled=True)
    returned = returned.reshape(pools * slots, share)
    moe = jnp.dot(take_high, returned, preferred_element_type=F32) + jnp.dot(
        take_low, returned, preferred_element_type=F32
    )
    return (hidden + moe).astype(BF16)


def solution(mesh):
    placed = (
        P("pool", None),
        P("pool", "head"),
        P("pool", "head", None, None),
        P("pool", "head", None, None),
        P("pool", "head"),
        P("pool", "head"),
        P("pool"),
        P("head", None),
        P(),
        P("pool", None),
        P("pool", None),
        P("pool", None, "head"),
        P("pool", None, "head"),
        P("pool", "head", None),
    )
    return jax.shard_map(
        body, mesh=mesh, in_specs=placed, out_specs=P("pool", "head"), check_vma=False
    )
```

```python
import jax
import jax.numpy as jnp
from jax import lax
from jax.experimental import pallas as pl
from jax.experimental.pallas import tpu as pltpu
from jax.sharding import PartitionSpec as P


F32 = jnp.float32
BF16 = jnp.bfloat16
GROUP = 8
HEAD, ROW, COLUMN, CORE = range(4)
NEAR_ORDER = (2, 1, 3, 0)
FAR_ORDER = ((2, 0), (2, 1), (1, 0), (3, 0), (1, 1), (3, 1), (0, 1), (0, 0))


def attend_kernel(lengths, place, q_ref, k_hbm, v_hbm, nk_ref, nv_ref, proj_hbm, *outs):
    *out_refs, k_ref, v_ref, rows_ref, proj_ref, sum_ref, cache_sems, proj_sems = outs
    steps, parts = cache_sems.shape[1], proj_sems.shape[0]
    depth = proj_ref.shape[0] // parts

    def cached(g, kind):
        cut = pl.ds(g * GROUP, GROUP)
        source, target = ((k_hbm, k_ref), (v_hbm, v_ref))[kind]
        return pltpu.make_async_copy(source.at[cut, 0], target.at[cut], cache_sems.at[kind, g])

    def part(i):
        cut = pl.ds(i * depth, depth)
        return pltpu.make_async_copy(proj_hbm.at[cut], proj_ref.at[cut], proj_sems.at[i])

    for g in range(steps):
        for kind in range(2):
            cached(g, kind).start()
    for g in range(steps):
        for kind in range(2):
            cached(g, kind).wait()
        part(g).start()
        attend_group(g * GROUP, lengths, q_ref, k_ref, v_ref, nk_ref, nv_ref, rows_ref)
    attn = rows_ref[...].astype(BF16)
    groups = len(out_refs)
    share = out_refs[0].shape[1]
    for i in range(parts):
        part(i).wait()
        cut = slice(i * depth, (i + 1) * depth)
        for ahead in range(groups):
            column = lax.rem(place[HEAD] + ahead, groups) * share
            weight = proj_ref[cut, pl.ds(pl.multiple_of(column, share), share)]
            terms = jnp.dot(attn[:, cut], weight, preferred_element_type=F32)
            if i:
                terms = terms + sum_ref[ahead]
            if i < parts - 1:
                sum_ref[ahead] = terms
            else:
                out_refs[ahead][...] = terms.astype(out_refs[ahead].dtype)


def attend_group(base, lengths, q_ref, k_ref, v_ref, nk_ref, nv_ref, rows_ref):
    size = nk_ref.shape[1]
    heads = q_ref.shape[1] // size
    slots = k_ref.shape[1]
    scale = size ** (-0.5)
    queries = q_ref[pl.ds(base, GROUP), :].astype(F32)
    new_keys = nk_ref[pl.ds(base, GROUP), :].astype(F32)
    new_values = nv_ref[pl.ds(base, GROUP), :].astype(F32)
    slot_of = lax.broadcasted_iota(jnp.int32, (heads, slots), 1)
    blank = jnp.zeros((heads, size), F32)
    split = [
        jnp.concatenate([queries[j : j + 1, i * size : (i + 1) * size] for i in range(heads)], 0)
        for j in range(GROUP)
    ]
    scores = []
    for j in range(0, GROUP, 2):
        spread = jnp.concatenate(
            [jnp.concatenate([split[j], blank], 1), jnp.concatenate([blank, split[j + 1]], 1)], 0
        )
        keys = jnp.concatenate([k_ref[base + j], k_ref[base + j + 1]], 1)
        scores.append(
            lax.dot_general(
                spread.astype(BF16), keys, (((1,), (1,)), ((), ())), preferred_element_type=F32
            )
        )
    scores = jnp.concatenate(scores, 0) * scale
    new_keys, new_values = (
        jnp.concatenate([jnp.broadcast_to(new[j : j + 1], (heads, size)) for j in range(GROUP)], 0)
        for new in (new_keys, new_values)
    )
    fresh = jnp.sum(jnp.concatenate(split, 0) * new_keys, 1, keepdims=True) * scale
    live = jnp.concatenate([slot_of < lengths[base + j] for j in range(GROUP)], 0)
    scores = jnp.where(live, scores, -1e30)
    highest = jnp.maximum(jnp.max(scores, 1, keepdims=True), fresh)
    weights = jnp.where(live, jnp.exp(scores - highest), 0.0)
    own = jnp.exp(fresh - highest)
    total = jnp.sum(weights, 1, keepdims=True) + own
    share = 1.0 / total
    probs = (weights * share).astype(BF16)
    own = (own * share).astype(BF16).astype(F32) * new_values
    mixed = []
    for j in range(0, GROUP, 2):
        values = jnp.concatenate([v_ref[base + j], v_ref[base + j + 1]], 1)
        rows = slice(j * heads, (j + 2) * heads)
        pair = jnp.dot(probs[rows], values, preferred_element_type=F32)
        mixed += [pair[:heads, :size], pair[heads:, size:]]
    done = []
    for j in range(GROUP):
        mix = mixed[j] + own[j * heads : (j + 1) * heads]
        done.append(jnp.concatenate([mix[i : i + 1] for i in range(heads)], 1))
    rows_ref[pl.ds(base, GROUP), :] = jnp.concatenate(done, 0)


def in_hbm(value):
    return pltpu.with_memory_space_constraint(value, pltpu.HBM)


def in_vmem(values):
    return [pltpu.with_memory_space_constraint(value, pltpu.VMEM) for value in values]


def attend_project(query, key_cache, value_cache, new_key, new_value, lengths, place, out_proj, groups):
    rows, wide = query.shape
    size = new_key.shape[1]
    slots = key_cache.shape[2]
    share = out_proj.shape[1] // groups
    vmem = pl.BlockSpec(memory_space=pltpu.VMEM)
    smem = pl.BlockSpec(memory_space=pltpu.SMEM)
    hbm = pl.BlockSpec(memory_space=pl.ANY)
    return pl.pallas_call(
        attend_kernel,
        out_shape=[
            jax.ShapeDtypeStruct((rows, share), BF16 if ahead else F32) for ahead in range(groups)
        ],
        in_specs=[smem, smem, vmem, hbm, hbm, vmem, vmem, hbm],
        out_specs=[vmem] * groups,
        scratch_shapes=[
            pltpu.VMEM((rows, slots, size), BF16),
            pltpu.VMEM((rows, slots, size), BF16),
            pltpu.VMEM((rows, wide), F32),
            pltpu.VMEM(out_proj.shape, BF16),
            pltpu.VMEM((groups, rows, share), F32),
            pltpu.SemaphoreType.DMA((2, rows // GROUP)),
            pltpu.SemaphoreType.DMA((rows // GROUP,)),
        ],
        compiler_params=pltpu.CompilerParams(vmem_limit_bytes=24 << 20),
        name="attend_project",
    )(
        in_hbm(lengths),
        place,
        in_hbm(query),
        in_hbm(key_cache),
        in_hbm(value_cache),
        in_hbm(new_key),
        in_hbm(new_value),
        in_hbm(out_proj),
    )


def norm_kernel(place, own_ref, *refs):
    *other_refs, gain_ref, ids_ref, first_ref, second_ref = refs
    groups = 1 + len(other_refs)
    rows, share = own_ref.shape
    blocks = [own_ref[...]] + [ref[...].astype(F32) for ref in other_refs]
    square = sum(jnp.sum(block * block, 1, keepdims=True) for block in blocks)
    inverse = lax.rsqrt(square / (groups * share) + 1e-06)
    half = groups // 2
    for back, block in enumerate(blocks):
        gain = gain_ref[lax.rem(place[HEAD] + groups - back, groups)]
        out_ref = (first_ref, second_ref)[back // half]
        cut = (back % half) * share
        out_ref[:rows, cut : cut + share] = (block * inverse * gain).astype(BF16)
    for out_ref in (first_ref, second_ref):
        out_ref[rows:, :] = jnp.zeros((ids_ref.shape[0], half * share), BF16)
        out_ref[rows:, : ids_ref.shape[1]] = ids_ref[...]


def norm_rows(own, others, norm_gain, ids, place):
    rows, share = own.shape
    groups = 1 + len(others)
    gains = norm_gain.reshape(groups, 1, share)
    shape = jax.ShapeDtypeStruct((rows + ids.shape[0], groups // 2 * share), BF16)
    vmem = pl.BlockSpec(memory_space=pltpu.VMEM)
    return pl.pallas_call(
        norm_kernel,
        out_shape=[shape, shape],
        in_specs=[pl.BlockSpec(memory_space=pltpu.SMEM)] + [vmem] * (groups + 2),
        out_specs=[vmem, vmem],
        compiler_params=pltpu.CompilerParams(vmem_limit_bytes=8 << 20),
        name="norm_rows",
    )(place, *in_vmem([own, *others]), gains, ids)


def pick_kernel(place, *refs):
    count = 4
    pools = (place[ROW], place[COLUMN], place[CORE])
    slots, near, cores = refs[-1].shape[0], count, 2
    targets = count * cores
    depth = 32
    lanes = near * depth
    total = targets * slots
    line = lax.broadcasted_iota(jnp.int32, (total, lanes), 0)
    lane = lax.broadcasted_iota(jnp.int32, (total, lanes), 1)
    step, flip = line >> 7, (line >> 6) & 1
    expert, source, rank = (line >> 5) & 1, (line >> 3) & 3, line & 7
    core = pools[2] ^ flip
    upper_line = lax.broadcasted_iota(jnp.int32, (lanes, lanes), 0)
    upper_lane = lax.broadcasted_iota(jnp.int32, (lanes, lanes), 1)
    earlier = ((upper_line < upper_lane) & ((upper_line >> 5) == (upper_lane >> 5))).astype(F32)
    id_lane = lax.broadcasted_iota(jnp.int32, (8, lanes), 1) >> 5
    for half in range(2):
        ins = [refs[2 * NEAR_ORDER.index(back) + half] for back in range(near)]
        outs = refs[(2 + 2 * half) * near : (4 + 2 * half) * near]
        if half == 0:
            target = ((pools[0] + step) & 3) * 8 + pools[1] * 2 + core
        else:
            target = pools[0] * 8 + ((pools[1] + step) & 3) * 2 + core
        wanted = (target * 2 + expert).astype(F32)
        ids = jnp.zeros((8, lanes), F32)
        for back, ref in enumerate(ins):
            ids = jnp.where(id_lane == back, ref[depth:, :lanes].astype(F32), ids)
        hit = ids[0:1] == wanted
        for k in range(1, 8):
            hit = hit | (ids[k : k + 1] == wanted)
        hits = jnp.where(hit, 1.0, 0.0).astype(BF16)
        order = jnp.dot(hits, earlier.astype(BF16), preferred_element_type=F32)
        chosen = hit & (order == rank.astype(F32)) & ((lane >> 5) == source)
        table = jnp.where(chosen, 1.0, 0.0).astype(BF16)
        rows = jnp.concatenate([ref[:depth, :] for ref in ins], 0)
        picked = jnp.dot(table, rows, preferred_element_type=F32).astype(BF16)
        for i, out_ref in enumerate(outs):
            out_ref[...] = picked[i * slots : (i + 1) * slots]


def pick_rows(first, second, place):
    width = first[0].shape[1]
    shape = jax.ShapeDtypeStruct((64, width), BF16)
    vmem = pl.BlockSpec(memory_space=pltpu.VMEM)
    out = pl.pallas_call(
        pick_kernel,
        out_shape=[shape] * 16,
        in_specs=[pl.BlockSpec(memory_space=pltpu.SMEM)] + [vmem] * 8,
        out_specs=[vmem] * 16,
        compiler_params=pltpu.CompilerParams(vmem_limit_bytes=16 << 20),
        name="pick_rows",
    )(place, *in_vmem([part[back] for back in NEAR_ORDER for part in (first, second)]))
    return out[:8], out[8:]


def load_kernel(*refs):
    *ins, first_sem = refs
    count = len(ins) // 2
    copies = [
        pltpu.make_async_copy(source.at[e], target.at[e], first_sem.at[i, e])
        for i, (source, target) in enumerate(zip(ins[:count], ins[count:]))
        for e in range(source.shape[0])
    ]
    for copy in copies:
        copy.start()
    for copy in copies:
        copy.wait()


def load(*values):
    return pl.pallas_call(
        load_kernel,
        out_shape=[pltpu.VMEM(value.shape, value.dtype) for value in values],
        in_specs=[pl.BlockSpec(memory_space=pl.ANY)] * len(values),
        out_specs=[pl.BlockSpec(memory_space=pltpu.VMEM)] * len(values),
        scratch_shapes=[pltpu.SemaphoreType.DMA((len(values), values[0].shape[0]))],
        compiler_params=pltpu.CompilerParams(vmem_limit_bytes=1 << 20),
        name="load",
    )(*[in_hbm(value) for value in values])


def gate_up_kernel(place, *refs):
    first, second = [None] * 8, [None] * 8
    for i, (step, flip) in enumerate(FAR_ORDER):
        first[step * 2 + flip], second[step * 2 + flip] = refs[2 * i : 2 * i + 2]
    gate_ref, up_ref, act_ref, sum_ref = refs[16:]
    experts, width, units = gate_ref.shape
    share = first[0].shape[1] // 2
    groups = width // share
    rows = act_ref.shape[1]
    kinds = 2
    half = groups // 2
    for e in range(experts):
        sums = {}
        for back in range(groups):
            source = (first, second)[back // half]
            cut = slice((back % half) * share, (back % half + 1) * share)
            x = jnp.concatenate([ref[e * 32 : (e + 1) * 32, cut] for ref in source], 0)
            depth = lax.rem(place[HEAD] + groups - back, groups) * share
            depth = pl.ds(pl.multiple_of(depth, share), share)
            for kind, ref in enumerate((gate_ref, up_ref)):
                term = jnp.dot(x, ref[e, depth, :], preferred_element_type=F32)
                key = (kind, back // half)
                sums[key] = sums[key] + term if key in sums else term
        for dy in range(4):
            for dc in range(2):
                for dx in range(4):
                    pool = (
                        ((place[ROW] + 4 - dy) & 3) * 8
                        + ((place[COLUMN] + 4 - dx) & 3) * 2
                        + (place[CORE] ^ dc)
                    )
                    a = ((dy * 2 + dc) * 4 + dx) * 8
                    b = ((dx * 2 + dc) * 4 + dy) * 8
                    for kind in range(kinds):
                        sum_ref[kind, pool] = (
                            sums[kind, 0][a : a + 8] + sums[kind, 1][b : b + 8]
                        )
        gate = sum_ref[0].reshape(rows, units)
        up = sum_ref[1].reshape(rows, units)
        act_ref[e] = (gate / (1.0 + jnp.exp(-gate)) * up).astype(act_ref.dtype)


def gate_up(first, second, w_gate, w_up, place, pools, capacity):
    experts, _, units = w_gate.shape
    rows = pools * capacity
    vmem = pl.BlockSpec(memory_space=pltpu.VMEM)
    return pl.pallas_call(
        gate_up_kernel,
        out_shape=jax.ShapeDtypeStruct((experts, rows, units), BF16),
        in_specs=[pl.BlockSpec(memory_space=pltpu.SMEM)] + [vmem] * 18,
        out_specs=vmem,
        scratch_shapes=[pltpu.VMEM((2, pools, capacity, units), F32)],
        compiler_params=pltpu.CompilerParams(vmem_limit_bytes=12 << 20),
        name="gate_up",
    )(place, *in_vmem([part[step * 2 + flip] for step, flip in FAR_ORDER for part in (first, second)]), *in_vmem([w_gate, w_up]))


def down_kernel(place, *refs):
    *ins, out_ref = refs
    count = len(ins) // 2
    total = 0.0
    for act_ref, weight_ref in zip(ins[:count], ins[count:]):
        total = total + jnp.dot(act_ref[0], weight_ref[0], preferred_element_type=F32)
    out_ref[...] = total.astype(out_ref.dtype).reshape(out_ref.shape)


def down(acts, w_down, moved, place, pools, capacity):
    experts, rows, units = acts[0].shape
    share = moved[0].shape[2]
    return pl.pallas_call(
        down_kernel,
        out_shape=jax.ShapeDtypeStruct((pools, experts * capacity, share), BF16),
        grid_spec=pltpu.PrefetchScalarGridSpec(
            num_scalar_prefetch=1,
            grid=(experts,),
            in_specs=[pl.BlockSpec((1, rows, units), lambda e, p: (e, 0, 0))] * len(acts)
            + [pl.BlockSpec((1, units, share), lambda e, p: (e, 0, p[HEAD]))]
            + [pl.BlockSpec((1, units, share), lambda e, p: (e, 0, 0))] * len(moved),
            out_specs=pl.BlockSpec((pools, capacity, share), lambda e, p: (0, e, 0)),
        ),
        compiler_params=pltpu.CompilerParams(
            dimension_semantics=("arbitrary",), vmem_limit_bytes=16 << 20
        ),
        name="down",
    )(place, *in_vmem(acts), in_hbm(w_down), *in_vmem(moved))


def route_slots(expert_ids, capacity):
    flat = expert_ids.reshape(-1)
    order = jnp.arange(flat.shape[0])
    earlier = (flat[:, None] == flat[None, :]) & (order[None, :] < order[:, None])
    rank = jnp.sum(earlier.astype(jnp.int32), 1)
    return (flat * capacity + rank).reshape(expert_ids.shape)


def turned(value, step):
    groups = lax.axis_size("head")
    return lax.ppermute(value, "head", [(i, (i + step) % groups) for i in range(groups)])


def moved_in_plane(value, dy, dx, dc):
    pairs = []
    for y in range(4):
        for x in range(4):
            for c in range(2):
                to = (y + dy) % 4 * 8 + (x + dx) % 4 * 2 + (c ^ dc)
                pairs.append((y * 8 + x * 2 + c, to))
    return lax.ppermute(value, "pool", pairs)


def body(
    x_rows,
    query,
    key_cache,
    value_cache,
    new_key,
    new_value,
    lengths,
    out_proj,
    norm_gain,
    expert_ids,
    gate_weights,
    w_gate,
    w_up,
    w_down,
):
    pools = lax.axis_size("pool")
    groups = lax.axis_size("head")
    rows, width = x_rows.shape
    share = width // groups
    experts = w_gate.shape[0]
    capacity = max(2, 2 * expert_ids.shape[0] * expert_ids.shape[1] // (pools * experts))
    slots = experts * capacity
    head = lax.axis_index("head")
    steps = range(1, groups)

    pool = lax.axis_index("pool")
    place = jnp.stack([head, pool >> 3, (pool >> 1) & 3, pool & 1]).astype(jnp.int32)
    own, *away = attend_project(
        query, key_cache, value_cache, new_key, new_value, lengths, place, out_proj, groups
    )
    others = [turned(piece, step) for step, piece in zip(steps, away)]
    slot = route_slots(expert_ids, capacity)
    matching = jnp.arange(pools * slots)[:, None, None] == slot[None, :, :]
    take = jnp.sum(jnp.where(matching, gate_weights[None, :, :], 0.0), 2).T
    take_high = take.astype(BF16)
    take_low = (take - take_high.astype(F32)).astype(BF16)
    ids = jnp.tile(expert_ids.T.astype(BF16), (1, 128 // rows))
    columns = [
        lax.dynamic_slice_in_dim(w_down, lax.rem(head + step, groups) * share, share, 2)
        for step in steps
    ]
    others, columns = lax.optimization_barrier((others, columns))
    hidden = lax.dynamic_slice_in_dim(x_rows, head * share, share, 1).astype(F32) + own
    for other in others:
        hidden = hidden + other.astype(F32)
    slices = [turned(hidden.astype(BF16), step) for step in steps]
    moved = [turned(piece, step) for step, piece in zip(steps, columns)]
    first, second = norm_rows(hidden, slices, norm_gain, ids, place)
    along_x = [first] + [moved_in_plane(first, 0, step, 0) for step in (1, 2, 3)]
    along_y = [second] + [moved_in_plane(second, step, 0, 0) for step in (1, 2, 3)]
    for_y, for_x = pick_rows(along_x, along_y, place)
    ways = [(step, flip) for step in range(4) for flip in range(2)]
    from_y, from_x = list(for_y), list(for_x)
    for step, flip in FAR_ORDER[:-1]:
        way = ways.index((step, flip))
        from_y[way] = moved_in_plane(for_y[way], step, 0, flip)
        from_x[way] = moved_in_plane(for_x[way], 0, step, flip)
    gate_near, up_near = load(w_gate, w_up)
    act = gate_up(from_y, from_x, gate_near, up_near, place, pools, capacity)
    acts = [act] + [turned(act, step) for step in steps]
    produced = down(acts, w_down, moved, place, pools, capacity)
    returned = lax.all_to_all(produced, "pool", split_axis=0, concat_axis=0, tiled=True)
    returned = returned.reshape(pools * slots, share)
    moe = jnp.dot(take_high, returned, preferred_element_type=F32) + jnp.dot(
        take_low, returned, preferred_element_type=F32
    )
    return (hidden + moe).astype(BF16)


def solution(mesh):
    placed = (
        P("pool", None),
        P("pool", "head"),
        P("pool", "head", None, None),
        P("pool", "head", None, None),
        P("pool", "head"),
        P("pool", "head"),
        P("pool"),
        P("head", None),
        P(),
        P("pool", None),
        P("pool", None),
        P("pool", None, "head"),
        P("pool", None, "head"),
        P("pool", "head", None),
    )
    return jax.shard_map(
        body, mesh=mesh, in_specs=placed, out_specs=P("pool", "head"), check_vma=False
    )
```
